32 devices in a mesh: dp: 8 (over z, core), seq: 4 (over y, x).
Axes of the slice: x: 2, y: 2, z: 4, core: 2. Of those that a mesh axis runs over, the one named last changes fastest.
Arguments:
- hidden: bfloat16 [8, 2, 256, 8192], P('dp', None, 'seq'), may hold values from -6 to 6
- queries: bfloat16 [8, 2, 256, 4096], P('dp', None, 'seq'), may hold values from -240 to 240
- key_matrix: bfloat16 [8192, 1024], P('dp', 'seq'), may hold values from -0.0625 to 0.0625
- value_matrix: bfloat16 [8192, 1024], P('dp', 'seq'), may hold values from -0.0625 to 0.0625
- out_grad: bfloat16 [8, 2, 256, 4096], P('dp', None, 'seq'), may hold values from -6 to 6
Outputs:
- attn_out: bfloat16 [8, 2, 256, 4096], P('dp', None, 'seq')
- query_grad: bfloat16 [8, 2, 256, 4096], P('dp', None, 'seq')
- key_weight_grad: float32 [8192, 1024], P('dp', 'seq')
- value_weight_grad: float32 [8192, 1024], P('dp', 'seq')
The draws below stay inside these ranges and needn't reach their ends.
All inputs are finite; a program needn't handle non-finite values.
Results may differ from the reference program's by a relative error of at most 0.025.
The reference program's roundings to bfloat16 on the way count: a program that leaves them out, or rounds other values in their place, can miss the bound.
Values may be sent and summed in bfloat16 or wider, within the bound.
A program may use at most 128 MiB of HBM per device.

```python
import math
import jax
import jax.numpy as jnp
from jax import lax

EMBED_WIDTH = 8192
QUERY_HEADS_HALF = 32
KEY_VALUE_HEADS = 8
HEAD_WIDTH = 128
STRETCHES = 2
STRETCH = 256
BATCH = 8


def draw_queries(key, part):
    base_key = jax.random.fold_in(jax.random.fold_in(key, 7), 0)
    base = jax.random.truncated_normal(base_key, -6.0, 6.0, (BATCH, STRETCHES, STRETCH, QUERY_HEADS_HALF * HEAD_WIDTH), jnp.float32)
    return base.astype(jnp.bfloat16)


def block_levels(key, shape, cuts, low, top_value):
    loudness, own = 1.0, jax.random.fold_in(key, 6)
    for position, shards_of in cuts:
        steps = jnp.exp(jax.random.uniform(jax.random.fold_in(own, position), (shards_of,), jnp.float32, low / len(cuts), top_value / len(cuts)))
        loudness = loudness * jnp.repeat(steps, shape[position] // shards_of).reshape([-1 if axis == position else 1 for axis in range(len(shape))])
    return loudness


def scatter_about(own_key, shape, width, reach, pieces=(), held_as=jnp.bfloat16):
    entries = jax.random.normal(own_key, shape, jnp.float32) * width
    if len(pieces) > 0:
        entries = block_levels(own_key, shape, pieces, -0.22, 0.18) * entries
    return jnp.clip(entries, min=-reach, max=reach).astype(held_as)


def setup_inputs(seed: int = 0) -> dict:
    key_of = jax.random.split(jax.random.key(seed), 6)
    return {
        "hidden": scatter_about(key_of[0], (BATCH, STRETCHES, STRETCH, EMBED_WIDTH), 1.0, 6.0, ((0, 8), (2, 4))),
        "queries": draw_queries(jax.random.fold_in(key_of[5], 71), 0),
        "key_matrix": scatter_about(key_of[2], (EMBED_WIDTH, KEY_VALUE_HEADS * HEAD_WIDTH), EMBED_WIDTH ** -0.5, 0.0625, ((0, 8), (1, 4))),
        "value_matrix": scatter_about(key_of[3], (EMBED_WIDTH, KEY_VALUE_HEADS * HEAD_WIDTH), EMBED_WIDTH ** -0.5, 0.0625, ((0, 8), (1, 4))),
        "out_grad": scatter_about(key_of[4], (BATCH, STRETCHES, STRETCH, QUERY_HEADS_HALF * HEAD_WIDTH), 1.0, 6.0, ((0, 8), (2, 4))),
    }


ROPE_BASE = 500000.0

def angle_tables(count, model_head):
    places = jnp.arange(count, dtype=jnp.float32)
    inverse = jnp.exp(jnp.arange(model_head // 2, dtype=jnp.float32) * (-2.0 * math.log(ROPE_BASE) / model_head))
    phase_table = places[:, None] * inverse[None, :]
    return (jnp.cos(phase_table), jnp.sin(phase_table))

def rotate(vector, cosine_lookup, sine_lookup):
    half_width = vector.shape[-1] // 2
    first_half = vector[..., :half_width]
    second_half = vector[..., half_width:]
    return jnp.concatenate([first_half * cosine_lookup - second_half * sine_lookup, second_half * cosine_lookup + first_half * sine_lookup], axis=-1)

def unrotate_gradient(vector, cosine_lookup, sine_lookup):
    half_width = vector.shape[-1] // 2
    first_half = vector[..., :half_width]
    second_half = vector[..., half_width:]
    return jnp.concatenate([first_half * cosine_lookup + second_half * sine_lookup, second_half * cosine_lookup - first_half * sine_lookup], axis=-1)

def reference(hidden, queries, key_matrix, value_matrix, out_grad):
    heads_per_group = QUERY_HEADS_HALF // KEY_VALUE_HEADS
    combined_length = STRETCHES * STRETCH
    score_scale = 1.0 / math.sqrt(HEAD_WIDTH)
    cosine_lookup, sine_lookup = angle_tables(combined_length, HEAD_WIDTH)
    cosine_lookup = cosine_lookup[:, None, :]
    sine_lookup = sine_lookup[:, None, :]
    allowed = jnp.arange(combined_length)[None, :] <= jnp.arange(combined_length)[:, None]

    def one_sequence(running, inputs):
        token_inputs, query_sequence, gradient_sequence = inputs
        token_inputs = token_inputs.reshape(combined_length, EMBED_WIDTH)
        query_whole = query_sequence.reshape(combined_length, KEY_VALUE_HEADS, heads_per_group, HEAD_WIDTH).astype(jnp.float32)
        gradient_whole = gradient_sequence.reshape(combined_length, KEY_VALUE_HEADS, heads_per_group, HEAD_WIDTH).astype(jnp.float32)
        key_projected_raw = jnp.dot(token_inputs, key_matrix, preferred_element_type=jnp.float32).reshape(combined_length, KEY_VALUE_HEADS, HEAD_WIDTH)
        key_half = rotate(key_projected_raw, cosine_lookup, sine_lookup).astype(jnp.bfloat16)
        key_cache = lax.optimization_barrier(key_half).astype(jnp.float32)
        value_stretch_half = jnp.dot(token_inputs, value_matrix, preferred_element_type=jnp.float32).astype(jnp.bfloat16)
        cached_values = lax.optimization_barrier(value_stretch_half).astype(jnp.float32).reshape(combined_length, KEY_VALUE_HEADS, HEAD_WIDTH)
        scores = jnp.einsum('tkgd,skd->kgts', query_whole, key_cache) * score_scale
        scores = jnp.where(allowed[None, None], scores, -jnp.inf)
        row_peak = lax.optimization_barrier(jnp.max(scores, axis=-1, keepdims=True))
        exp_scores = jnp.exp(scores - row_peak)
        prob_full = exp_scores / lax.optimization_barrier(jnp.sum(exp_scores, axis=-1, keepdims=True))
        prob_half = lax.optimization_barrier(prob_full.astype(jnp.bfloat16)).astype(jnp.float32)
        attended = jnp.einsum('kgts,skd->tkgd', prob_half, cached_values).astype(jnp.bfloat16)
        attended_wide = lax.optimization_barrier(attended).astype(jnp.float32)
        grad_prob = jnp.einsum('tkgd,skd->kgts', gradient_whole, cached_values)
        row_dot = jnp.einsum('tkgd,tkgd->kgt', gradient_whole, attended_wide)
        grad_score = (prob_full * (grad_prob - row_dot[..., None]) * score_scale).astype(jnp.bfloat16)
        grad_score = lax.optimization_barrier(grad_score).astype(jnp.float32)
        query_grad_seq = jnp.einsum('kgts,skd->tkgd', grad_score, key_cache).astype(jnp.bfloat16)
        key_gradient = jnp.einsum('kgts,tkgd->skd', grad_score, query_whole)
        value_gradient = jnp.einsum('kgts,tkgd->skd', prob_half, gradient_whole)
        key_unrotated = unrotate_gradient(key_gradient, cosine_lookup, sine_lookup).astype(jnp.bfloat16).reshape(combined_length, KEY_VALUE_HEADS * HEAD_WIDTH)
        value_projected = value_gradient.astype(jnp.bfloat16).reshape(combined_length, KEY_VALUE_HEADS * HEAD_WIDTH)
        key_term = jnp.dot(token_inputs.T, key_unrotated, preferred_element_type=jnp.float32)
        value_term = jnp.dot(token_inputs.T, value_projected, preferred_element_type=jnp.float32)
        outputs = (attended.reshape(STRETCHES, STRETCH, QUERY_HEADS_HALF * HEAD_WIDTH), query_grad_seq.reshape(STRETCHES, STRETCH, QUERY_HEADS_HALF * HEAD_WIDTH))
        return ((running[0] + key_term, running[1] + value_term), outputs)
    leading_gradients = (jnp.zeros((EMBED_WIDTH, KEY_VALUE_HEADS * HEAD_WIDTH), jnp.float32), jnp.zeros((EMBED_WIDTH, KEY_VALUE_HEADS * HEAD_WIDTH), jnp.float32))
    (key_weight_grad, value_weight_grad), (attn_out, query_grad) = lax.scan(one_sequence, leading_gradients, (hidden, queries, out_grad))
    return (attn_out, query_grad, key_weight_grad, value_weight_grad)
```

```python
import functools
import math

import jax
import jax.numpy as jnp
import numpy as np
from jax import lax
from jax.experimental import pallas as pl
from jax.experimental.pallas import tpu as pltpu
from jax.sharding import PartitionSpec as P

HEAD_WIDTH = 128
ROPE_BASE = 500000.0
CORES = 2
MESH = pl.DeviceIdType.MESH
ANY = pl.BlockSpec(memory_space=pl.ANY)
VMEM = pl.BlockSpec(memory_space=pltpu.VMEM)
VMEM_LIMIT = 56 << 20


def grid_of(count):
    rows = 2 if count % 2 == 0 else 1
    return rows, count // rows


def place(n_seq, n_dp):
    dp, seq = lax.axis_index("dp"), lax.axis_index("seq")
    chips = n_dp // CORES
    chip, core = lax.div(dp, CORES), lax.rem(dp, CORES)
    rows, cols = grid_of(n_seq)
    row, col = lax.div(seq, cols), lax.rem(seq, cols)
    row_peers = [row * cols + lax.rem(col + d, cols) for d in range(1, cols)]
    col_peers = [lax.rem(row + d, rows) * cols + col for d in range(1, rows)]
    far_peers = [
        lax.rem(row + e, rows) * cols + lax.rem(col + d, cols)
        for e in range(1, rows)
        for d in range(1, cols)
    ]
    return dp, seq, chips, chip, core, row_peers, col_peers, far_peers


def kernel(
    n_seq, n_dp, kv_heads, group, tile,
    hidden, queries, key_matrix, value_matrix, out_grad, cos, sin, cos_t, sin_t,
    attn_out, qgrad_out, key_grad, val_grad,
    hid, qry, grd, key_all, val_all, raw_k, raw_v, own_k, own_v, out_k, out_v, in_k, in_v,
    keys, vals, attn, qgrad, pre_t, pre_in,
    key_acc, val_acc, acc, mate_out, mate_in, far_out, far_in,
    load_sem, own_sem, store_sem, hid_send, hid_recv, qry_send, qry_recv, grd_send, grd_recv,
    far_w_send, mate_w_send, w_recv, k_send, k_recv, v_send, v_recv, pre_send, pre_recv,
    a_send, a_recv, q_send, q_recv, mate_send, mate_recv, far_send, far_recv,
):
    f32, bf16 = jnp.float32, jnp.bfloat16
    dp, seq, chips, chip, core, row_peers, col_peers, far_peers = place(n_seq, n_dp)
    peers = row_peers + col_peers + far_peers
    near = chips // 2
    side, slot_w = lax.div(chip, near), lax.rem(chip, near)
    mate = chip * CORES + 1 - core
    twin = ((1 - side) * near + slot_w) * CORES + core
    others = [lax.rem(slot_w + d, near) for d in range(1, near)]

    def owner(w):
        return (side * near + w) * CORES + core

    wide = group * HEAD_WIDTH
    width = kv_heads * wide
    total = keys.shape[0]
    half = HEAD_WIDTH // 2
    block = total // 2
    deep = key_all.shape[1]
    quarter = hid.shape[-1]
    per = quarter // deep
    mine = slot_w * CORES + core

    barrier = pltpu.get_barrier_semaphore()
    greeted = [(dp, p) for p in peers] + [(mate, seq), (twin, seq)]
    greeted += [(owner(w), seq) for w in others]
    for device in greeted:
        pl.semaphore_signal(barrier, inc=1, device_id=device, device_id_type=MESH)
    pl.semaphore_wait(barrier, len(greeted))

    def head_cols(target, kv):
        return pl.ds(pl.multiple_of(target * width + kv * wide, wide), wide)

    def one_head(target, h):
        start = pl.multiple_of(target * width + h * HEAD_WIDTH, HEAD_WIDTH)
        return pl.ds(start, HEAD_WIDTH)

    def embed_cols(which, j):
        return pl.ds(pl.multiple_of((which * 2 + j) * quarter, quarter), quarter)

    loads = [
        (hidden.at[:, :, embed_cols(side, j)], hid.at[0, j, :, seq], load_sem.at[j])
        for j in range(2)
    ] + [
        (key_matrix, key_all.at[mine], load_sem.at[2]),
        (value_matrix, val_all.at[mine], load_sem.at[3]),
    ]

    def own_loads(h):
        return (
            (queries.at[:, :, one_head(seq, h)], qry.at[h, :, seq], own_sem.at[0, h]),
            (out_grad.at[:, :, one_head(seq, h)], grd.at[h, :, seq], own_sem.at[1, h]),
        )

    sends = []

    def start(copy):
        copy.start()
        sends.append(copy)

    slots = iter(range(hid_send.shape[0]))

    def hidden_copy(slot, e, j, source, target_dp, target, src, send_sem):
        return pltpu.make_async_remote_copy(
            src_ref=src, dst_ref=hid.at[slot, j, e, source],
            send_sem=send_sem, recv_sem=hid_recv.at[slot, e, j, source],
            device_id=(target_dp, target), device_id_type=MESH,
        )

    def send_hidden(slot, e, j, source, target, own=False):
        src = hidden.at[e, :, embed_cols(side, j)] if own else hid.at[slot, j, e, source]
        start(hidden_copy(slot, e, j, source, dp, target, src, hid_send.at[next(slots)]))

    def wait_hidden(slot, e, j, source):
        src = hid.at[slot, j, e, source]
        hidden_copy(slot, e, j, source, dp, source, src, hid_send.at[0]).wait_recv()

    def direct(slot, e):
        own = slot == 0
        for first, second, j_pair in ((row_peers, col_peers, (0, 1)), (row_peers, col_peers, (1, 0))):
            for p in first:
                send_hidden(slot, e, j_pair[0], seq, p, own)
            for p in second:
                send_hidden(slot, e, j_pair[1], seq, p, own)

    def relay_hidden(slot, e):
        for p in row_peers:
            wait_hidden(slot, e, 0, p)
            for q in col_peers:
                send_hidden(slot, e, 0, p, q)
        for p in col_peers:
            wait_hidden(slot, e, 1, p)
            for q in row_peers:
                send_hidden(slot, e, 1, p, q)

    def wait_rest(slot, e):
        for p in row_peers:
            wait_hidden(slot, e, 1, p)
        for p in col_peers:
            wait_hidden(slot, e, 0, p)
        for p in far_peers:
            wait_hidden(slot, e, 0, p)
            wait_hidden(slot, e, 1, p)

    def arrive(e):
        for j in range(2):
            src = hid.at[1, j, e, seq]
            hidden_copy(1, e, j, seq, twin, seq, src, hid_send.at[0]).wait_recv()

    tables = (key_all, val_all)
    owns = (key_matrix, value_matrix)

    def weight_copy(kind, piece, target_dp, send_sem, own=False):
        return pltpu.make_async_remote_copy(
            src_ref=owns[kind] if own else tables[kind].at[piece],
            dst_ref=tables[kind].at[piece],
            send_sem=send_sem, recv_sem=w_recv.at[piece, kind],
            device_id=(target_dp, seq), device_id_type=MESH,
        )

    def relay_weights():
        for i, w in enumerate(others):
            for kind in range(2):
                piece = w * CORES + core
                weight_copy(kind, piece, owner(w), far_w_send.at[i, kind]).wait_recv()
                start(weight_copy(kind, piece, mate, mate_w_send.at[i + 1, kind]))

    def wait_weights():
        for w in [slot_w] + others:
            for kind in range(2):
                piece = w * CORES + 1 - core
                weight_copy(kind, piece, mate, mate_w_send.at[0, kind]).wait_recv()

    def exchange(h, src, dst, send_sem, recv_sem):
        for i, p in enumerate(peers):
            start(pltpu.make_async_remote_copy(
                src_ref=src.at[:, :, one_head(p, h)], dst_ref=dst.at[h, :, seq],
                send_sem=send_sem.at[h, i], recv_sem=recv_sem.at[h, seq],
                device_id=(dp, p), device_id_type=MESH,
            ))

    def wait_exchange(h, dst, send_sem, recv_sem):
        for p in peers:
            pltpu.make_async_remote_copy(
                src_ref=dst.at[h, :, p], dst_ref=dst.at[h, :, p],
                send_sem=send_sem.at[h, 0], recv_sem=recv_sem.at[h, p],
                device_id=(dp, p), device_id_type=MESH,
            ).wait_recv()

    def project(slot, e):
        raw_k[...] = jnp.zeros_like(raw_k)
        raw_v[...] = jnp.zeros_like(raw_v)

        @pl.loop(0, 2 * per)
        def _(i):
            j, at = lax.div(i, per), lax.rem(i, per)
            cols = pl.ds(pl.multiple_of(at * deep, deep), deep)
            rows = hid[slot, j, e, :, :, cols].reshape(block, deep)
            raw_k[...] += jnp.dot(rows, key_all[i], preferred_element_type=f32)
            raw_v[...] += jnp.dot(rows, val_all[i], preferred_element_type=f32)

        for kv in range(kv_heads):
            lanes = pl.ds(kv * HEAD_WIDTH, HEAD_WIDTH)
            to_k, to_v = (own_k, own_v) if slot == 0 else (out_k, out_v)
            to_k[kv, e] = raw_k[:, lanes].astype(to_k.dtype)
            to_v[kv, e] = raw_v[:, lanes].astype(to_v.dtype)

    def raw_copies(kv, e):
        return [
            pltpu.make_async_remote_copy(
                src_ref=src.at[kv, e], dst_ref=dst.at[kv, e],
                send_sem=send_sem.at[kv, e], recv_sem=recv_sem.at[kv, e],
                device_id=(twin, seq), device_id_type=MESH,
            )
            for src, dst, send_sem, recv_sem in (
                (out_k, in_k, k_send, k_recv), (out_v, in_v, v_send, v_recv),
            )
        ]

    def send_raw(e):
        for kv in range(kv_heads):
            for copy in raw_copies(kv, e):
                start(copy)

    def settle(kv, e):
        lanes = pl.ds(kv * HEAD_WIDTH, HEAD_WIDTH)
        rows = pl.ds(e * block, block)
        for copy in raw_copies(kv, e):
            copy.wait_recv()
        raw = own_k[kv, e] + in_k[kv, e]
        swapped = jnp.concatenate([raw[:, half:], raw[:, :half]], axis=1)
        keys[rows, lanes] = (raw * cos[rows, :] + swapped * sin[rows, :]).astype(bf16)
        vals[rows, lanes] = (own_v[kv, e] + in_v[kv, e].astype(f32)).astype(bf16)

    scale = 1.0 / math.sqrt(HEAD_WIDTH)
    nt = (((1,), (1,)), ((), ()))
    tn = (((0,), (0,)), ((), ()))

    def attend(kv):
        lanes = pl.ds(kv * HEAD_WIDTH, HEAD_WIDTH)
        key_acc[...] = jnp.zeros_like(key_acc)
        val_acc[...] = jnp.zeros_like(val_acc)

        @pl.loop(0, group)
        def _(m):
            head = pl.ds(pl.multiple_of(m * HEAD_WIDTH, HEAD_WIDTH), HEAD_WIDTH)
            h = kv * group + m
            wait_exchange(h, qry, qry_send, qry_recv)
            wait_exchange(h, grd, grd_send, grd_recv)
            for copy in own_loads(h):
                pltpu.make_async_copy(*copy).wait()
            for b in range(2):
                span = (b + 1) * block
                q = qry[h, b].reshape(block, HEAD_WIDTH)
                g = grd[h, b].reshape(block, HEAD_WIDTH)
                k, v = keys[:span, lanes], vals[:span, lanes]
                s = lax.dot_general(q, k, nt, preferred_element_type=f32) * scale
                at = b * block + lax.broadcasted_iota(jnp.int32, s.shape, 0)
                col = lax.broadcasted_iota(jnp.int32, s.shape, 1)
                s = jnp.where(col <= at, s, -jnp.inf)
                e = jnp.exp(s - jnp.max(s, axis=1, keepdims=True))
                p = e * (1.0 / jnp.sum(e, axis=1, keepdims=True))
                p_half = p.astype(bf16)
                o = jnp.dot(p_half, v, preferred_element_type=f32).astype(bf16)
                attn[kv, b, :, :, head] = o.reshape(n_seq, block // n_seq, HEAD_WIDTH)
                dot = jnp.sum(g.astype(f32) * o.astype(f32), axis=1, keepdims=True)
                gp = lax.dot_general(g, v, nt, preferred_element_type=f32)
                ds = (p * (gp - dot) * scale).astype(bf16)
                dq = jnp.dot(ds, k, preferred_element_type=f32).astype(bf16)
                qgrad[kv, b, :, :, head] = dq.reshape(n_seq, block // n_seq, HEAD_WIDTH)
                key_acc[:, :span] += lax.dot_general(q, ds, tn, preferred_element_type=f32)
                val_acc[:, :span] += lax.dot_general(g, p_half, tn, preferred_element_type=f32)

        grown = key_acc[...]
        swapped = jnp.concatenate([grown[half:, :], grown[:half, :]], axis=0)
        pre_t[kv, :HEAD_WIDTH, :] = (grown * cos_t[...] - swapped * sin_t[...]).astype(bf16)
        pre_t[kv, HEAD_WIDTH:, :] = val_acc[...].astype(bf16)

    def pre_copy(kv):
        return pltpu.make_async_remote_copy(
            src_ref=pre_t.at[kv], dst_ref=pre_in.at[kv],
            send_sem=pre_send.at[kv], recv_sem=pre_recv.at[kv],
            device_id=(twin, seq), device_id_type=MESH,
        )

    height, depth = acc.shape[2], acc.shape[3]
    results = ((attn, attn_out, a_send, a_recv), (qgrad, qgrad_out, q_send, q_recv))

    def own_store(kv, which):
        src, dst, _, _ = results[which]
        return pltpu.make_async_copy(
            src.at[kv, :, seq], dst.at[:, :, head_cols(seq, kv)], store_sem.at[which, kv]
        )

    def give_back(kv):
        for which, (src, dst, send_sem, recv_sem) in enumerate(results):
            for i, p in enumerate(peers):
                start(pltpu.make_async_remote_copy(
                    src_ref=src.at[kv, :, p], dst_ref=dst.at[:, :, head_cols(seq, kv)],
                    send_sem=send_sem.at[kv, i], recv_sem=recv_sem.at[kv, seq],
                    device_id=(dp, p), device_id_type=MESH,
                ))
            own_store(kv, which).start()

    def wait_back(kv):
        for which, (src, dst, send_sem, recv_sem) in enumerate(results):
            for p in peers:
                pltpu.make_async_remote_copy(
                    src_ref=src.at[kv, :, p], dst_ref=dst.at[:, :, head_cols(p, kv)],
                    send_sem=send_sem.at[kv, 0], recv_sem=recv_sem.at[kv, p],
                    device_id=(dp, p), device_id_type=MESH,
                ).wait_recv()
            own_store(kv, which).wait()

    def mate_copy(kv, w):
        return pltpu.make_async_remote_copy(
            src_ref=mate_out.at[kv, w], dst_ref=mate_in.at[kv, w],
            send_sem=mate_send.at[kv, w], recv_sem=mate_recv.at[kv, w],
            device_id=(mate, seq), device_id_type=MESH,
        )

    def far_copy(kv, i, w):
        return pltpu.make_async_remote_copy(
            src_ref=far_out.at[kv, i], dst_ref=far_in.at[kv, slot_w],
            send_sem=far_send.at[kv, i], recv_sem=far_recv.at[kv, slot_w],
            device_id=(owner(w), seq), device_id_type=MESH,
        )

    def wait_far(kv, i, w):
        pltpu.make_async_remote_copy(
            src_ref=far_out.at[kv, i], dst_ref=far_in.at[kv, w],
            send_sem=far_send.at[kv, i], recv_sem=far_recv.at[kv, w],
            device_id=(owner(w), seq), device_id_type=MESH,
        ).wait_recv()

    def product(kv, piece, store):
        j, at = lax.div(piece, per), lax.rem(piece, per)

        @pl.loop(0, depth // tile)
        def _(i):
            cols = pl.ds(pl.multiple_of(at * depth + i * tile, tile), tile)
            part = jnp.dot(
                pre_t[kv], hid[0, j, :, :, :, cols].reshape(total, tile),
                preferred_element_type=f32,
            )
            part += jnp.dot(
                pre_in[kv], hid[1, j, :, :, :, cols].reshape(total, tile),
                preferred_element_type=f32,
            )
            store(pl.ds(pl.multiple_of(i * tile, tile), tile), part)

    strip = 32

    def sweep(fn):
        @pl.loop(0, height // strip)
        def _(i):
            fn(pl.ds(pl.multiple_of(i * strip, strip), strip))

    def products(kv):
        def to_mate(w):
            def store(cols, part):
                mate_out[kv, w, :, cols] = part.astype(bf16)

            product(kv, w * CORES + 1 - core, store)
            start(mate_copy(kv, w))

        def to_acc(w):
            def store(cols, part):
                acc[kv, w, :, cols] = part

            product(kv, w * CORES + core, store)

        pre_copy(kv).wait_recv()
        for w in others:
            to_mate(w)
        for w in others:
            to_acc(w)
        to_mate(slot_w)
        for i, w in enumerate(others):
            mate_copy(kv, w).wait_recv()

            def fn(rows):
                v = acc[kv, w, rows, :] + mate_in[kv, w, rows, :].astype(f32)
                far_out[kv, i, rows, :] = v.astype(bf16)

            sweep(fn)
            start(far_copy(kv, i, w))
        to_acc(slot_w)

    def finish(kv):
        lanes = pl.ds(kv * HEAD_WIDTH, HEAD_WIDTH)
        mate_copy(kv, slot_w).wait_recv()
        for i, w in enumerate(others):
            wait_far(kv, i, w)

        @pl.loop(0, depth // HEAD_WIDTH)
        def _(j):
            at = pl.ds(pl.multiple_of(j * HEAD_WIDTH, HEAD_WIDTH), HEAD_WIDTH)
            v = acc[kv, slot_w, :, at] + mate_in[kv, slot_w, :, at].astype(f32)
            for w in others:
                v = v + far_in[kv, w, :, at].astype(f32)
            key_grad[at, lanes] = v[:HEAD_WIDTH, :].T
            val_grad[at, lanes] = v[HEAD_WIDTH:, :].T

    for e in range(2):
        for j in range(2):
            src = hidden.at[e, :, embed_cols(1 - side, j)]
            start(hidden_copy(1, e, j, seq, twin, seq, src, hid_send.at[next(slots)]))
    direct(0, 0)
    for kind in range(2):
        for i, w in enumerate(others):
            start(weight_copy(kind, mine, owner(w), far_w_send.at[i, kind], True))
        start(weight_copy(kind, mine, mate, mate_w_send.at[0, kind], True))
    for copy in loads:
        pltpu.make_async_copy(*copy).start()
    direct(0, 1)
    for h in range(kv_heads * group):
        for copy in own_loads(h):
            pltpu.make_async_copy(*copy).start()
    relay_hidden(0, 0)
    relay_hidden(0, 1)
    arrive(0)
    direct(1, 0)
    relay_weights()
    for copy in loads:
        pltpu.make_async_copy(*copy).wait()
    wait_weights()
    wait_rest(0, 0)
    project(0, 0)
    relay_hidden(1, 0)
    arrive(1)
    direct(1, 1)
    wait_rest(0, 1)
    project(0, 1)
    wait_rest(1, 0)
    project(1, 0)
    send_raw(0)
    relay_hidden(1, 1)
    for h in range(kv_heads * group):
        exchange(h, queries, qry, qry_send, qry_recv)
        exchange(h, out_grad, grd, grd_send, grd_recv)
    wait_rest(1, 1)
    project(1, 1)
    send_raw(1)
    for kv in range(kv_heads):
        settle(kv, 0)
        settle(kv, 1)
        attend(kv)
        start(pre_copy(kv))
        give_back(kv)
    for kv in range(kv_heads):
        products(kv)
    for kv in range(kv_heads):
        finish(kv)
        wait_back(kv)
    for copy in sends:
        copy.wait_send()


def put_kernel(*refs):
    count = len(refs) // 2
    sem = refs[-1]
    copies = [
        pltpu.make_async_copy(refs[i], refs[count + i], sem.at[i]) for i in range(count)
    ]
    for copy in copies:
        copy.start()
    for copy in copies:
        copy.wait()


def put_all(*arrays):
    return pl.pallas_call(
        put_kernel,
        out_shape=[jax.ShapeDtypeStruct(x.shape, x.dtype) for x in arrays],
        in_specs=[pl.BlockSpec(memory_space=pltpu.VMEM)] * len(arrays),
        out_specs=[ANY] * len(arrays),
        scratch_shapes=[pltpu.SemaphoreType.DMA((len(arrays),))],
        compiler_params=pltpu.CompilerParams(vmem_limit_bytes=1 << 20),
        name="put_all",
    )(*arrays)


def local(n_seq, n_dp, hidden, queries, key_matrix, value_matrix, out_grad):
    _, stretches, tokens, embed = hidden.shape
    full = queries.shape[3]
    width = full // n_seq
    deep, kv_width = key_matrix.shape
    kv_heads = kv_width // HEAD_WIDTH
    group = width // kv_width
    wide = group * HEAD_WIDTH
    near = n_dp // CORES // 2
    quarter = embed // 4
    rows, cols = grid_of(n_seq)
    hid_sends = 4 * (2 * (rows - 1 + cols - 1) + 2 * (rows - 1) * (cols - 1)) + 4
    total = stretches * n_seq * tokens
    block = n_seq * tokens
    bf16, f32 = jnp.bfloat16, jnp.float32
    dma = pltpu.SemaphoreType.DMA
    half = HEAD_WIDTH // 2
    inverse = np.exp(
        np.arange(half, dtype=np.float32) * np.float32(-2.0 * math.log(ROPE_BASE) / HEAD_WIDTH)
    ).astype(np.float32)
    phase = np.arange(total, dtype=np.float32)[:, None] * inverse[None, :]
    cos_half, sin_half = np.cos(phase), np.sin(phase)
    cos = np.concatenate([cos_half, cos_half], axis=1).astype(np.float32)
    sin = np.concatenate([-sin_half, sin_half], axis=1).astype(np.float32)
    heads = (kv_heads, stretches, n_seq, tokens, wide)
    single = (kv_heads * group, stretches, n_seq, tokens, HEAD_WIDTH)
    height = 2 * HEAD_WIDTH
    blocks = (kv_heads, near, height, deep)
    weights = (n_dp // 2, deep, kv_width)
    raw = (kv_heads, stretches, block, HEAD_WIDTH)
    all_heads = kv_heads * group
    spare = max(near - 1, 1)
    attn_out, query_grad, key_grad, val_grad = pl.pallas_call(
        functools.partial(kernel, n_seq, n_dp, kv_heads, group, math.gcd(deep, 256)),
        out_shape=[
            pltpu.VMEM((stretches, tokens, full), bf16),
            pltpu.VMEM((stretches, tokens, full), bf16),
            pltpu.VMEM((deep, kv_width), f32),
            pltpu.VMEM((deep, kv_width), f32),
        ],
        in_specs=[ANY] * 5 + [VMEM] * 4,
        out_specs=[VMEM] * 4,
        scratch_shapes=[
            pltpu.VMEM((2, 2, stretches, n_seq, tokens, quarter), bf16),
            pltpu.VMEM(single, bf16),
            pltpu.VMEM(single, bf16),
            pltpu.VMEM(weights, bf16),
            pltpu.VMEM(weights, bf16),
            pltpu.VMEM((block, kv_width), f32),
            pltpu.VMEM((block, kv_width), f32),
            pltpu.VMEM(raw, f32),
            pltpu.VMEM(raw, f32),
            pltpu.VMEM(raw, f32),
            pltpu.VMEM(raw, bf16),
            pltpu.VMEM(raw, f32),
            pltpu.VMEM(raw, bf16),
            pltpu.VMEM((total, kv_width), bf16),
            pltpu.VMEM((total, kv_width), bf16),
            pltpu.VMEM(heads, bf16),
            pltpu.VMEM(heads, bf16),
            pltpu.VMEM((kv_heads, height, total), bf16),
            pltpu.VMEM((kv_heads, height, total), bf16),
            pltpu.VMEM((HEAD_WIDTH, total), f32),
            pltpu.VMEM((HEAD_WIDTH, total), f32),
            pltpu.VMEM(blocks, f32),
            pltpu.VMEM(blocks, bf16),
            pltpu.VMEM(blocks, bf16),
            pltpu.VMEM((kv_heads, spare, height, deep), bf16),
            pltpu.VMEM(blocks, bf16),
            dma((4,)), dma((2, all_heads)), dma((2, kv_heads)),
            dma((hid_sends,)), dma((2, stretches, 2, n_seq)),
            dma((all_heads, n_seq)), dma((all_heads, n_seq)),
            dma((all_heads, n_seq)), dma((all_heads, n_seq)),
            dma((spare, 2)), dma((near, 2)), dma((n_dp // 2, 2)),
            dma((kv_heads, stretches)), dma((kv_heads, stretches)),
            dma((kv_heads, stretches)), dma((kv_heads, stretches)),
            dma((kv_heads,)), dma((kv_heads,)),
            dma((kv_heads, n_seq)), dma((kv_heads, n_seq)),
            dma((kv_heads, n_seq)), dma((kv_heads, n_seq)),
            dma((kv_heads, near)), dma((kv_heads, near)),
            dma((kv_heads, spare)), dma((kv_heads, near)),
        ],
        compiler_params=pltpu.CompilerParams(
            collective_id=0, has_side_effects=True, vmem_limit_bytes=VMEM_LIMIT
        ),
        name="attention_step",
    )(hidden[0], queries[0], key_matrix, value_matrix, out_grad[0],
      cos, sin, cos.T.copy(), sin.T.copy())
    attn_out, query_grad, key_grad, val_grad = put_all(
        attn_out, query_grad, key_grad, val_grad
    )
    return attn_out[None], query_grad[None], key_grad, val_grad


def solution(mesh):
    n_dp, n_seq = mesh.shape["dp"], mesh.shape["seq"]
    tokens, weights = P("dp", None, "seq", None), P("dp", "seq")
    return jax.shard_map(
        functools.partial(local, n_seq, n_dp),
        mesh=mesh,
        in_specs=(tokens, tokens, weights, weights, tokens),
        out_specs=(tokens, tokens, weights, weights),
        check_vma=False,
    )
```

```python
import functools
import math

import jax
import jax.numpy as jnp
import numpy as np
from jax import lax
from jax.experimental import pallas as pl
from jax.experimental.pallas import tpu as pltpu
from jax.sharding import PartitionSpec as P

HEAD_WIDTH = 128
ROPE_BASE = 500000.0
CORES = 2
MESH = pl.DeviceIdType.MESH
ANY = pl.BlockSpec(memory_space=pl.ANY)
VMEM = pl.BlockSpec(memory_space=pltpu.VMEM)
VMEM_LIMIT = 56 << 20


def grid_of(count):
    rows = 2 if count % 2 == 0 else 1
    return rows, count // rows


def place(n_seq, n_dp):
    dp, seq = lax.axis_index("dp"), lax.axis_index("seq")
    chips = n_dp // CORES
    chip, core = lax.div(dp, CORES), lax.rem(dp, CORES)
    rows, cols = grid_of(n_seq)
    row, col = lax.div(seq, cols), lax.rem(seq, cols)
    row_peers = [row * cols + lax.rem(col + d, cols) for d in range(1, cols)]
    col_peers = [lax.rem(row + d, rows) * cols + col for d in range(1, rows)]
    far_peers = [
        lax.rem(row + e, rows) * cols + lax.rem(col + d, cols)
        for e in range(1, rows)
        for d in range(1, cols)
    ]
    return dp, seq, chips, chip, core, row_peers, col_peers, far_peers


def kernel(
    n_seq, n_dp, kv_heads, group, tile,
    hidden, queries, key_matrix, value_matrix, out_grad, cos, sin, cos_t, sin_t,
    attn_out, qgrad_out, key_grad, val_grad,
    hid, qry, grd, key_all, val_all, sum_k, sum_v, raw_k, raw_v, raw_h, in_k, in_v,
    keys, vals, attn, qgrad, pre_t, pre_in,
    key_acc, val_acc, acc, mate_acc, mate_out, mate_in, far_out, far_in,
    load_sem, own_sem, store_sem, hid_send, hid_recv, qry_send, qry_recv, grd_send, grd_recv,
    far_w_send, mate_w_send, w_recv, k_send, k_recv, v_send, v_recv, pre_send, pre_recv,
    a_send, a_recv, q_send, q_recv, mate_send, mate_recv, far_send, far_recv,
):
    f32, bf16 = jnp.float32, jnp.bfloat16
    dp, seq, chips, chip, core, row_peers, col_peers, far_peers = place(n_seq, n_dp)
    peers = row_peers + col_peers + far_peers
    near = chips // 2
    side, slot_w = lax.div(chip, near), lax.rem(chip, near)
    mate = chip * CORES + 1 - core
    twin = ((1 - side) * near + slot_w) * CORES + core
    others = [lax.rem(slot_w + d, near) for d in range(1, near)]

    def owner(w):
        return (side * near + w) * CORES + core

    wide = group * HEAD_WIDTH
    width = kv_heads * wide
    total = keys.shape[0]
    half = HEAD_WIDTH // 2
    block = total // 2
    deep = key_all.shape[1]
    quarter = hid.shape[-1]
    per = quarter // deep
    mine = slot_w * CORES + core
    tokens = hid.shape[4]
    piece_len = tokens // 2
    is_end = jnp.logical_or(chip == 0, chip == chips - 1).astype(jnp.int32)

    def turn(p):
        if p == 0:
            return 0, 0
        outer = (1, p - 1) if p <= 4 else (0, p - 4)
        inner = (0, p) if p <= 3 else (1, p - 4)
        return tuple(is_end * a + (1 - is_end) * b for a, b in zip(outer, inner))

    def stretch_of(c):
        e, u = (c // 2, c % 2) if isinstance(c, int) else (lax.div(c, 2), lax.rem(c, 2))
        start = u * piece_len
        return e, pl.ds(start if isinstance(c, int) else pl.multiple_of(start, piece_len), piece_len)

    barrier = pltpu.get_barrier_semaphore()
    greeted = [(dp, p) for p in peers] + [(mate, seq), (twin, seq)]
    greeted += [(owner(w), seq) for w in others]
    for device in greeted:
        pl.semaphore_signal(barrier, inc=1, device_id=device, device_id_type=MESH)
    pl.semaphore_wait(barrier, len(greeted))

    def head_cols(target, kv):
        return pl.ds(pl.multiple_of(target * width + kv * wide, wide), wide)

    def one_head(target, h):
        start = pl.multiple_of(target * width + h * HEAD_WIDTH, HEAD_WIDTH)
        return pl.ds(start, HEAD_WIDTH)

    def embed_cols(which, j):
        return pl.ds(pl.multiple_of((which * 2 + j) * quarter, quarter), quarter)

    loads = [
        (key_matrix, key_all.at[mine], load_sem.at[0]),
        (value_matrix, val_all.at[mine], load_sem.at[1]),
    ]
    for c in range(4):
        e, at = stretch_of(c)
        for j in range(2):
            pltpu.make_async_copy(
                hidden.at[e, at, embed_cols(side, j)], hid.at[0, j, e, seq, at],
                hid_recv.at[0, c, j, seq],
            ).start()

    def own_loads(h):
        return (
            (queries.at[:, :, one_head(seq, h)], qry.at[h, :, seq], own_sem.at[0, h]),
            (out_grad.at[:, :, one_head(seq, h)], grd.at[h, :, seq], own_sem.at[1, h]),
        )

    sends = []

    def start(copy):
        copy.start()
        sends.append(copy)

    slots = iter(range(hid_send.shape[0]))

    def hidden_copy(slot, c, j, source, target_dp, target, send_sem, src=None):
        e, at = stretch_of(c)
        dst = hid.at[slot, j, e, source, at]
        return pltpu.make_async_remote_copy(
            src_ref=dst if src is None else src, dst_ref=dst,
            send_sem=send_sem, recv_sem=hid_recv.at[slot, c, j, source],
            device_id=(target_dp, target), device_id_type=MESH,
        )

    def send_hidden(slot, c, j, source, target):
        start(hidden_copy(slot, c, j, source, dp, target, hid_send.at[next(slots)]))

    def wait_hidden(slot, c, j, source):
        hidden_copy(slot, c, j, source, dp, source, hid_send.at[0]).wait_recv()

    def direct(p):
        slot, c = turn(p)
        for j in range(2):
            wait_hidden(slot, c, j, seq)
        for j in range(2):
            for q in row_peers:
                send_hidden(slot, c, j, seq, q)
            for q in col_peers:
                send_hidden(slot, c, 1 - j, seq, q)

    def relay_hidden(p):
        slot, c = turn(p)
        for r in row_peers:
            wait_hidden(slot, c, 0, r)
            for q in col_peers:
                send_hidden(slot, c, 0, r, q)
        for r in col_peers:
            wait_hidden(slot, c, 1, r)
            for q in row_peers:
                send_hidden(slot, c, 1, r, q)

    def wait_rest(p):
        slot, c = turn(p)
        for r in row_peers:
            wait_hidden(slot, c, 1, r)
        for r in col_peers:
            wait_hidden(slot, c, 0, r)
        for r in far_peers:
            wait_hidden(slot, c, 0, r)
            wait_hidden(slot, c, 1, r)

    tables = (key_all, val_all)
    owns = (key_matrix, value_matrix)

    def weight_copy(kind, piece, target_dp, send_sem, own=False):
        return pltpu.make_async_remote_copy(
            src_ref=owns[kind] if own else tables[kind].at[piece],
            dst_ref=tables[kind].at[piece],
            send_sem=send_sem, recv_sem=w_recv.at[piece, kind],
            device_id=(target_dp, seq), device_id_type=MESH,
        )

    def relay_weights():
        for i, w in enumerate(others):
            for kind in range(2):
                piece = w * CORES + core
                weight_copy(kind, piece, owner(w), far_w_send.at[i, kind]).wait_recv()
                start(weight_copy(kind, piece, mate, mate_w_send.at[i + 1, kind]))

    def wait_weights():
        for w in [slot_w] + others:
            for kind in range(2):
                piece = w * CORES + 1 - core
                weight_copy(kind, piece, mate, mate_w_send.at[0, kind]).wait_recv()

    def exchange(h, src, dst, send_sem, recv_sem):
        for i, p in enumerate(peers):
            start(pltpu.make_async_remote_copy(
                src_ref=src.at[:, :, one_head(p, h)], dst_ref=dst.at[h, :, seq],
                send_sem=send_sem.at[h, i], recv_sem=recv_sem.at[h, seq],
                device_id=(dp, p), device_id_type=MESH,
            ))

    def wait_exchange(h, dst, send_sem, recv_sem):
        for p in peers:
            pltpu.make_async_remote_copy(
                src_ref=dst.at[h, :, p], dst_ref=dst.at[h, :, p],
                send_sem=send_sem.at[h, 0], recv_sem=recv_sem.at[h, p],
                device_id=(dp, p), device_id_type=MESH,
            ).wait_recv()

    def project(p):
        slot, c = turn(p)
        e, at_rows = stretch_of(c)
        wait_rest(p)
        sum_k[...] = jnp.zeros_like(sum_k)
        sum_v[...] = jnp.zeros_like(sum_v)

        @pl.loop(0, 2 * per)
        def _(i):
            j, at = lax.div(i, per), lax.rem(i, per)
            cols = pl.ds(pl.multiple_of(at * deep, deep), deep)
            rows = hid[slot, j, e, :, at_rows, cols].reshape(n_seq * piece_len, deep)
            sum_k[...] += jnp.dot(rows, key_all[i], preferred_element_type=f32)
            sum_v[...] += jnp.dot(rows, val_all[i], preferred_element_type=f32)

        shape = (n_seq, piece_len, HEAD_WIDTH)
        for kv in range(kv_heads):
            lanes = pl.ds(kv * HEAD_WIDTH, HEAD_WIDTH)
            raw_k[slot, kv, e, :, at_rows, :] = sum_k[:, lanes].reshape(shape)
            raw_v[slot, kv, e, :, at_rows, :] = sum_v[:, lanes].reshape(shape)
            raw_h[slot, kv, e, :, at_rows, :] = sum_v[:, lanes].reshape(shape).astype(bf16)
        if p > 0:

            @pl.when(slot == 1)
            def _():
                for kv in range(kv_heads):
                    for copy in raw_copies(kv, c):
                        copy.start()

    def raw_copies(kv, c):
        e, at = stretch_of(c)
        return [
            pltpu.make_async_remote_copy(
                src_ref=src.at[1, kv, e, :, at], dst_ref=dst.at[kv, e, :, at],
                send_sem=send_sem.at[kv, c], recv_sem=recv_sem.at[kv, c],
                device_id=(twin, seq), device_id_type=MESH,
            )
            for src, dst, send_sem, recv_sem in (
                (raw_k, in_k, k_send, k_recv), (raw_h, in_v, v_send, v_recv),
            )
        ]

    def settle(kv):
        lanes = pl.ds(kv * HEAD_WIDTH, HEAD_WIDTH)
        for c in range(4):
            for copy in raw_copies(kv, c):
                copy.wait_recv()
        flat = (total, HEAD_WIDTH)
        raw = raw_k[0, kv].reshape(flat) + in_k[kv].reshape(flat)
        swapped = jnp.concatenate([raw[:, half:], raw[:, :half]], axis=1)
        keys[:, lanes] = (raw * cos[...] + swapped * sin[...]).astype(bf16)
        vals[:, lanes] = (raw_v[0, kv].reshape(flat) + in_v[kv].reshape(flat).astype(f32)).astype(bf16)

    scale = 1.0 / math.sqrt(HEAD_WIDTH)
    nt = (((1,), (1,)), ((), ()))
    tn = (((0,), (0,)), ((), ()))

    def attend(kv):
        lanes = pl.ds(kv * HEAD_WIDTH, HEAD_WIDTH)
        key_acc[...] = jnp.zeros_like(key_acc)
        val_acc[...] = jnp.zeros_like(val_acc)

        @pl.loop(0, group)
        def _(m):
            head = pl.ds(pl.multiple_of(m * HEAD_WIDTH, HEAD_WIDTH), HEAD_WIDTH)
            h = kv * group + m
            wait_exchange(h, qry, qry_send, qry_recv)
            wait_exchange(h, grd, grd_send, grd_recv)
            for copy in own_loads(h):
                pltpu.make_async_copy(*copy).wait()
            for b in range(2):
                span = (b + 1) * block
                q = qry[h, b].reshape(block, HEAD_WIDTH)
                g = grd[h, b].reshape(block, HEAD_WIDTH)
                k, v = keys[:span, lanes], vals[:span, lanes]
                s = lax.dot_general(q, k, nt, preferred_element_type=f32) * scale
                at = b * block + lax.broadcasted_iota(jnp.int32, s.shape, 0)
                col = lax.broadcasted_iota(jnp.int32, s.shape, 1)
                s = jnp.where(col <= at, s, -jnp.inf)
                e = jnp.exp(s - jnp.max(s, axis=1, keepdims=True))
                p = e * (1.0 / jnp.sum(e, axis=1, keepdims=True))
                p_half = p.astype(bf16)
                o = jnp.dot(p_half, v, preferred_element_type=f32).astype(bf16)
                attn[kv, b, :, :, head] = o.reshape(n_seq, block // n_seq, HEAD_WIDTH)
                dot = jnp.sum(g.astype(f32) * o.astype(f32), axis=1, keepdims=True)
                gp = lax.dot_general(g, v, nt, preferred_element_type=f32)
                ds = (p * (gp - dot) * scale).astype(bf16)
                dq = jnp.dot(ds, k, preferred_element_type=f32).astype(bf16)
                qgrad[kv, b, :, :, head] = dq.reshape(n_seq, block // n_seq, HEAD_WIDTH)
                key_acc[:, :span] += lax.dot_general(q, ds, tn, preferred_element_type=f32)
                val_acc[:, :span] += lax.dot_general(g, p_half, tn, preferred_element_type=f32)

        grown = key_acc[...]
        swapped = jnp.concatenate([grown[half:, :], grown[:half, :]], axis=0)
        pre_t[kv, :HEAD_WIDTH, :] = (grown * cos_t[...] - swapped * sin_t[...]).astype(bf16)
        pre_t[kv, HEAD_WIDTH:, :] = val_acc[...].astype(bf16)

    def pre_copy(kv):
        return pltpu.make_async_remote_copy(
            src_ref=pre_t.at[kv], dst_ref=pre_in.at[kv],
            send_sem=pre_send.at[kv], recv_sem=pre_recv.at[kv],
            device_id=(twin, seq), device_id_type=MESH,
        )

    height, depth = acc.shape[3], deep
    results = ((attn, attn_out, a_send, a_recv), (qgrad, qgrad_out, q_send, q_recv))

    def own_store(kv, which):
        src, dst, _, _ = results[which]
        return pltpu.make_async_copy(
            src.at[kv, :, seq], dst.at[:, :, head_cols(seq, kv)], store_sem.at[which, kv]
        )

    def give_back(kv):
        for which, (src, dst, send_sem, recv_sem) in enumerate(results):
            for i, p in enumerate(peers):
                start(pltpu.make_async_remote_copy(
                    src_ref=src.at[kv, :, p], dst_ref=dst.at[:, :, head_cols(seq, kv)],
                    send_sem=send_sem.at[kv, i], recv_sem=recv_sem.at[kv, seq],
                    device_id=(dp, p), device_id_type=MESH,
                ))
            own_store(kv, which).start()

    def wait_back(kv):
        for which, (src, dst, send_sem, recv_sem) in enumerate(results):
            for p in peers:
                pltpu.make_async_remote_copy(
                    src_ref=src.at[kv, :, p], dst_ref=dst.at[:, :, head_cols(p, kv)],
                    send_sem=send_sem.at[kv, 0], recv_sem=recv_sem.at[kv, p],
                    device_id=(dp, p), device_id_type=MESH,
                ).wait_recv()
            own_store(kv, which).wait()

    parts = depth // tile

    def mate_copy(kv, w, t):
        return pltpu.make_async_remote_copy(
            src_ref=mate_out.at[kv, w, t], dst_ref=mate_in.at[kv, w, t],
            send_sem=mate_send.at[kv, w, t], recv_sem=mate_recv.at[kv, w, t],
            device_id=(mate, seq), device_id_type=MESH,
        )

    def far_copy(kv, i, w, t, back=False):
        at = w if back else slot_w
        return pltpu.make_async_remote_copy(
            src_ref=far_out.at[kv, i, t], dst_ref=far_in.at[kv, at, t],
            send_sem=far_send.at[kv, i, t], recv_sem=far_recv.at[kv, at, t],
            device_id=(owner(w), seq), device_id_type=MESH,
        )

    def part_of(pre, kv, slot, piece, t):
        j, at = lax.div(piece, per), lax.rem(piece, per)
        cols = pl.ds(pl.multiple_of(at * depth + t * tile, tile), tile)
        rows = hid[slot, j, :, :, :, cols].reshape(total, tile)
        return jnp.dot(pre[kv], rows, preferred_element_type=f32)

    def own_products(kv):
        for w in others + [slot_w]:
            @pl.loop(0, parts)
            def _(t):
                mate_acc[kv, w, t] = part_of(pre_t, kv, 0, w * CORES + 1 - core, t)
                acc[kv, w, t] = part_of(pre_t, kv, 0, w * CORES + core, t)

    def twin_products(kv):
        def to_mate(w):
            @pl.loop(0, parts)
            def _(t):
                v = mate_acc[kv, w, t] + part_of(pre_in, kv, 1, w * CORES + 1 - core, t)
                mate_out[kv, w, t] = v.astype(bf16)
                mate_copy(kv, w, t).start()

        def to_acc(w):
            @pl.loop(0, parts)
            def _(t):
                acc[kv, w, t] += part_of(pre_in, kv, 1, w * CORES + core, t)

        pre_copy(kv).wait_recv()
        for w in others:
            to_mate(w)
        for w in others:
            to_acc(w)
        for i, w in enumerate(others):
            @pl.loop(0, parts)
            def _(t):
                mate_copy(kv, w, t).wait_recv()
                v = acc[kv, w, t] + mate_in[kv, w, t].astype(f32)
                far_out[kv, i, t] = v.astype(bf16)
                far_copy(kv, i, w, t).start()
        to_mate(slot_w)
        to_acc(slot_w)

        @pl.loop(0, parts)
        def _(t):
            mate_copy(kv, slot_w, t).wait_recv()
            acc[kv, slot_w, t] += mate_in[kv, slot_w, t].astype(f32)

    def finish(kv):
        lanes = pl.ds(kv * HEAD_WIDTH, HEAD_WIDTH)
        for t in range(parts):
            v = acc[kv, slot_w, t]
            for i, w in enumerate(others):
                far_copy(kv, i, w, t, True).wait_recv()
                v = v + far_in[kv, w, t].astype(f32)
            at = pl.ds(t * tile, tile)
            key_grad[at, lanes] = v[:HEAD_WIDTH, :].T
            val_grad[at, lanes] = v[HEAD_WIDTH:, :].T

    for kind in range(2):
        for i, w in enumerate(others):
            start(weight_copy(kind, mine, owner(w), far_w_send.at[i, kind], True))
        start(weight_copy(kind, mine, mate, mate_w_send.at[0, kind], True))
    for c in range(4):
        e, at = stretch_of(c)
        for j in range(2):
            src = hidden.at[e, at, embed_cols(1 - side, j)]
            start(hidden_copy(1, c, j, seq, twin, seq, hid_send.at[next(slots)], src))
    for copy in loads:
        pltpu.make_async_copy(*copy).start()
    direct(0)
    for h in range(kv_heads * group):
        for copy in own_loads(h):
            pltpu.make_async_copy(*copy).start()
    steps = 8
    for p in range(steps):
        if p + 1 < steps:
            direct(p + 1)
        relay_hidden(p)
        if p == 2:
            relay_weights()
        if p == 3:
            for copy in loads:
                pltpu.make_async_copy(*copy).wait()
            wait_weights()
            project(0)
            project(1)
        if p >= 3 and p + 1 < steps:
            project(p - 1)
    for h in range(kv_heads * group):
        exchange(h, queries, qry, qry_send, qry_recv)
        exchange(h, out_grad, grd, grd_send, grd_recv)
    project(steps - 2)
    project(steps - 1)
    for kv in range(kv_heads):
        settle(kv)
        attend(kv)
        start(pre_copy(kv))
        give_back(kv)
    for kv in range(kv_heads):
        own_products(kv)
        if kv > 0:
            twin_products(kv - 1)
    twin_products(kv_heads - 1)
    for kv in range(kv_heads):
        finish(kv)
        wait_back(kv)
    for kv in range(kv_heads):
        for c in range(4):
            for copy in raw_copies(kv, c):
                copy.wait_send()
        for t in range(parts):
            for w in range(near):
                mate_copy(kv, w, t).wait_send()
            for i, w in enumerate(others):
                far_copy(kv, i, w, t).wait_send()
    for copy in sends:
        copy.wait_send()


def put_kernel(*refs):
    count = len(refs) // 2
    sem = refs[-1]
    copies = [
        pltpu.make_async_copy(refs[i], refs[count + i], sem.at[i]) for i in range(count)
    ]
    for copy in copies:
        copy.start()
    for copy in copies:
        copy.wait()


def put_all(*arrays):
    return pl.pallas_call(
        put_kernel,
        out_shape=[jax.ShapeDtypeStruct(x.shape, x.dtype) for x in arrays],
        in_specs=[pl.BlockSpec(memory_space=pltpu.VMEM)] * len(arrays),
        out_specs=[ANY] * len(arrays),
        scratch_shapes=[pltpu.SemaphoreType.DMA((len(arrays),))],
        compiler_params=pltpu.CompilerParams(vmem_limit_bytes=1 << 20),
        name="put_all",
    )(*arrays)


def local(n_seq, n_dp, hidden, queries, key_matrix, value_matrix, out_grad):
    _, stretches, tokens, embed = hidden.shape
    full = queries.shape[3]
    width = full // n_seq
    deep, kv_width = key_matrix.shape
    kv_heads = kv_width // HEAD_WIDTH
    group = width // kv_width
    wide = group * HEAD_WIDTH
    near = n_dp // CORES // 2
    quarter = embed // 4
    rows, cols = grid_of(n_seq)
    hid_sends = 8 * (2 * (rows - 1 + cols - 1) + 2 * (rows - 1) * (cols - 1)) + 8
    total = stretches * n_seq * tokens
    block = n_seq * tokens
    bf16, f32 = jnp.bfloat16, jnp.float32
    dma = pltpu.SemaphoreType.DMA
    half = HEAD_WIDTH // 2
    inverse = np.exp(
        np.arange(half, dtype=np.float32) * np.float32(-2.0 * math.log(ROPE_BASE) / HEAD_WIDTH)
    ).astype(np.float32)
    phase = np.arange(total, dtype=np.float32)[:, None] * inverse[None, :]
    cos_half, sin_half = np.cos(phase), np.sin(phase)
    cos = np.concatenate([cos_half, cos_half], axis=1).astype(np.float32)
    sin = np.concatenate([-sin_half, sin_half], axis=1).astype(np.float32)
    heads = (kv_heads, stretches, n_seq, tokens, wide)
    single = (kv_heads * group, stretches, n_seq, tokens, HEAD_WIDTH)
    height = 2 * HEAD_WIDTH
    tile = math.gcd(deep, 256)
    parts = deep // tile
    blocks = (kv_heads, near, parts, height, tile)
    weights = (n_dp // 2, deep, kv_width)
    raw = (kv_heads, stretches, n_seq, tokens, HEAD_WIDTH)
    all_heads = kv_heads * group
    spare = max(near - 1, 1)
    attn_out, query_grad, key_grad, val_grad = pl.pallas_call(
        functools.partial(kernel, n_seq, n_dp, kv_heads, group, tile),
        out_shape=[
            pltpu.VMEM((stretches, tokens, full), bf16),
            pltpu.VMEM((stretches, tokens, full), bf16),
            pltpu.VMEM((deep, kv_width), f32),
            pltpu.VMEM((deep, kv_width), f32),
        ],
        in_specs=[ANY] * 5 + [VMEM] * 4,
        out_specs=[VMEM] * 4,
        scratch_shapes=[
            pltpu.VMEM((2, 2, stretches, n_seq, tokens, quarter), bf16),
            pltpu.VMEM(single, bf16),
            pltpu.VMEM(single, bf16),
            pltpu.VMEM(weights, bf16),
            pltpu.VMEM(weights, bf16),
            pltpu.VMEM((block // 2, kv_width), f32),
            pltpu.VMEM((block // 2, kv_width), f32),
            pltpu.VMEM((2,) + raw, f32),
            pltpu.VMEM((2,) + raw, f32),
            pltpu.VMEM((2,) + raw, bf16),
            pltpu.VMEM(raw, f32),
            pltpu.VMEM(raw, bf16),
            pltpu.VMEM((total, kv_width), bf16),
            pltpu.VMEM((total, kv_width), bf16),
            pltpu.VMEM(heads, bf16),
            pltpu.VMEM(heads, bf16),
            pltpu.VMEM((kv_heads, height, total), bf16),
            pltpu.VMEM((kv_heads, height, total), bf16),
            pltpu.VMEM((HEAD_WIDTH, total), f32),
            pltpu.VMEM((HEAD_WIDTH, total), f32),
            pltpu.VMEM(blocks, f32),
            pltpu.VMEM(blocks, f32),
            pltpu.VMEM(blocks, bf16),
            pltpu.VMEM(blocks, bf16),
            pltpu.VMEM((kv_heads, spare, parts, height, tile), bf16),
            pltpu.VMEM(blocks, bf16),
            dma((2,)), dma((2, all_heads)), dma((2, kv_heads)),
            dma((hid_sends,)), dma((2, 4, 2, n_seq)),
            dma((all_heads, n_seq)), dma((all_heads, n_seq)),
            dma((all_heads, n_seq)), dma((all_heads, n_seq)),
            dma((spare, 2)), dma((near, 2)), dma((n_dp // 2, 2)),
            dma((kv_heads, 4)), dma((kv_heads, 4)),
            dma((kv_heads, 4)), dma((kv_heads, 4)),
            dma((kv_heads,)), dma((kv_heads,)),
            dma((kv_heads, n_seq)), dma((kv_heads, n_seq)),
            dma((kv_heads, n_seq)), dma((kv_heads, n_seq)),
            dma((kv_heads, near, parts)), dma((kv_heads, near, parts)),
            dma((kv_heads, spare, parts)), dma((kv_heads, near, parts)),
        ],
        compiler_params=pltpu.CompilerParams(
            collective_id=0, has_side_effects=True, vmem_limit_bytes=VMEM_LIMIT
        ),
        name="attention_step",
    )(hidden[0], queries[0], key_matrix, value_matrix, out_grad[0],
      cos, sin, cos.T.copy(), sin.T.copy())
    attn_out, query_grad, key_grad, val_grad = put_all(
        attn_out, query_grad, key_grad, val_grad
    )
    return attn_out[None], query_grad[None], key_grad, val_grad


def solution(mesh):
    n_dp, n_seq = mesh.shape["dp"], mesh.shape["seq"]
    tokens, weights = P("dp", None, "seq", None), P("dp", "seq")
    return jax.shard_map(
        functools.partial(local, n_seq, n_dp),
        mesh=mesh,
        in_specs=(tokens, tokens, weights, weights, tokens),
        out_specs=(tokens, tokens, weights, weights),
        check_vma=False,
    )
```

```python
import functools
import math

import jax
import jax.numpy as jnp
import numpy as np
from jax import lax
from jax.experimental import pallas as pl
from jax.experimental.pallas import tpu as pltpu
from jax.sharding import PartitionSpec as P

HEAD_WIDTH = 128
ROPE_BASE = 500000.0
CORES = 2
MESH = pl.DeviceIdType.MESH
ANY = pl.BlockSpec(memory_space=pl.ANY)
VMEM = pl.BlockSpec(memory_space=pltpu.VMEM)
VMEM_LIMIT = 56 << 20


def grid_of(count):
    rows = 2 if count % 2 == 0 else 1
    return rows, count // rows


def place(n_seq, n_dp):
    dp, seq = lax.axis_index("dp"), lax.axis_index("seq")
    chips = n_dp // CORES
    chip, core = lax.div(dp, CORES), lax.rem(dp, CORES)
    rows, cols = grid_of(n_seq)
    row, col = lax.div(seq, cols), lax.rem(seq, cols)
    row_peers = [row * cols + lax.rem(col + d, cols) for d in range(1, cols)]
    col_peers = [lax.rem(row + d, rows) * cols + col for d in range(1, rows)]
    far_peers = [
        lax.rem(row + e, rows) * cols + lax.rem(col + d, cols)
        for e in range(1, rows)
        for d in range(1, cols)
    ]
    return dp, seq, chips, chip, core, row_peers, col_peers, far_peers


def kernel(
    n_seq, n_dp, kv_heads, group, tile,
    hidden, queries, key_matrix, value_matrix, out_grad, cos, sin, cos_t, sin_t,
    attn_out, qgrad_out, key_grad, val_grad,
    hid, qry, grd, key_all, val_all, sum_k, sum_v, raw_k, raw_v, raw_h, in_k, in_v,
    keys, vals, attn, qgrad, pre_t, pre_in,
    key_acc, val_acc, acc, mate_acc, mate_out, mate_in, far_out, far_in,
    load_sem, own_sem, store_sem, hid_send, hid_recv, qry_send, qry_recv, grd_send, grd_recv,
    far_w_send, far_w_recv, mate_w_send, w_recv, k_send, k_recv, v_send, v_recv, pre_send, pre_recv,
    a_send, a_recv, q_send, q_recv, mate_send, mate_recv, far_send, far_recv,
):
    f32, bf16 = jnp.float32, jnp.bfloat16
    dp, seq, chips, chip, core, row_peers, col_peers, far_peers = place(n_seq, n_dp)
    peers = row_peers + col_peers + far_peers
    near = chips // 2
    side, slot_w = lax.div(chip, near), lax.rem(chip, near)
    mate = chip * CORES + 1 - core
    twin = ((1 - side) * near + slot_w) * CORES + core
    others = [lax.rem(slot_w + d, near) for d in range(1, near)]

    def owner(w):
        return (side * near + w) * CORES + core

    wide = group * HEAD_WIDTH
    width = kv_heads * wide
    total = keys.shape[0]
    half = HEAD_WIDTH // 2
    block = total // 2
    deep = key_all.shape[1]
    quarter = hid.shape[-1]
    per = quarter // deep
    mine = slot_w * CORES + core
    tokens = hid.shape[4]
    piece_len = tokens // 2
    turns = ((0, 0), (0, 1), (1, 0), (0, 2), (1, 1), (1, 2), (1, 3), (0, 3))

    def stretch_of(c):
        return c // 2, pl.ds(c % 2 * piece_len, piece_len)

    barrier = pltpu.get_barrier_semaphore()
    greeted = [(dp, p) for p in peers] + [(mate, seq), (twin, seq)]
    greeted += [(owner(w), seq) for w in others]
    for device in greeted:
        pl.semaphore_signal(barrier, inc=1, device_id=device, device_id_type=MESH)
    pl.semaphore_wait(barrier, len(greeted))

    def head_cols(target, kv):
        return pl.ds(pl.multiple_of(target * width + kv * wide, wide), wide)

    def one_head(target, h):
        start = pl.multiple_of(target * width + h * HEAD_WIDTH, HEAD_WIDTH)
        return pl.ds(start, HEAD_WIDTH)

    def embed_cols(which, j):
        return pl.ds(pl.multiple_of((which * 2 + j) * quarter, quarter), quarter)

    loads = [
        (key_matrix, key_all.at[mine], load_sem.at[0]),
        (value_matrix, val_all.at[mine], load_sem.at[1]),
    ]
    for c in range(4):
        e, at = stretch_of(c)
        for j in range(2):
            pltpu.make_async_copy(
                hidden.at[e, at, embed_cols(side, j)], hid.at[0, j, e, seq, at],
                hid_recv.at[0, c, j, seq],
            ).start()

    def own_loads(h):
        return (
            (queries.at[:, :, one_head(seq, h)], qry.at[h, :, seq], own_sem.at[0, h]),
            (out_grad.at[:, :, one_head(seq, h)], grd.at[h, :, seq], own_sem.at[1, h]),
        )

    sends = []

    def start(copy):
        copy.start()
        sends.append(copy)

    slots = iter(range(hid_send.shape[0]))

    def hidden_copy(slot, c, j, source, target_dp, target, send_sem, src=None):
        e, at = stretch_of(c)
        dst = hid.at[slot, j, e, source, at]
        return pltpu.make_async_remote_copy(
            src_ref=dst if src is None else src, dst_ref=dst,
            send_sem=send_sem, recv_sem=hid_recv.at[slot, c, j, source],
            device_id=(target_dp, target), device_id_type=MESH,
        )

    def send_hidden(slot, c, j, source, target):
        start(hidden_copy(slot, c, j, source, dp, target, hid_send.at[next(slots)]))

    def wait_hidden(slot, c, j, source):
        hidden_copy(slot, c, j, source, dp, source, hid_send.at[0]).wait_recv()

    def direct(p):
        slot, c = turns[p]
        for j in range(2):
            wait_hidden(slot, c, j, seq)
        for j in range(2):
            for q in row_peers:
                send_hidden(slot, c, j, seq, q)
            for q in col_peers:
                send_hidden(slot, c, 1 - j, seq, q)

    def relay_hidden(p):
        slot, c = turns[p]
        for r in row_peers:
            wait_hidden(slot, c, 0, r)
            for q in col_peers:
                send_hidden(slot, c, 0, r, q)
        for r in col_peers:
            wait_hidden(slot, c, 1, r)
            for q in row_peers:
                send_hidden(slot, c, 1, r, q)

    def wait_rest(p):
        slot, c = turns[p]
        for r in row_peers:
            wait_hidden(slot, c, 1, r)
        for r in col_peers:
            wait_hidden(slot, c, 0, r)
        for r in far_peers:
            wait_hidden(slot, c, 0, r)
            wait_hidden(slot, c, 1, r)

    tables = (key_all, val_all)
    owns = (key_matrix, value_matrix)

    def weight_copy(kind, piece, target_dp, send_sem, own=False):
        return pltpu.make_async_remote_copy(
            src_ref=owns[kind] if own else tables[kind].at[piece],
            dst_ref=tables[kind].at[piece],
            send_sem=send_sem, recv_sem=w_recv.at[piece, kind],
            device_id=(target_dp, seq), device_id_type=MESH,
        )

    strip = deep // 4

    def far_weight(kind, r, i, w, source):
        at = pl.ds(r * strip, strip)
        return pltpu.make_async_remote_copy(
            src_ref=owns[kind].at[at], dst_ref=tables[kind].at[source * CORES + core, at],
            send_sem=far_w_send.at[i, kind, r], recv_sem=far_w_recv.at[source, kind, r],
            device_id=(owner(w), seq), device_id_type=MESH,
        )

    def relay_weights():
        for i, w in enumerate(others):
            for kind in range(2):
                for r in range(4):
                    far_weight(kind, r, i, w, w).wait_recv()
                start(weight_copy(kind, w * CORES + core, mate, mate_w_send.at[i + 1, kind]))

    def wait_weights():
        for w in [slot_w] + others:
            for kind in range(2):
                piece = w * CORES + 1 - core
                weight_copy(kind, piece, mate, mate_w_send.at[0, kind]).wait_recv()

    def exchange(h, src, dst, send_sem, recv_sem):
        for i, p in enumerate(peers):
            start(pltpu.make_async_remote_copy(
                src_ref=src.at[:, :, one_head(p, h)], dst_ref=dst.at[h, :, seq],
                send_sem=send_sem.at[h, i], recv_sem=recv_sem.at[h, seq],
                device_id=(dp, p), device_id_type=MESH,
            ))

    def wait_exchange(h, dst, send_sem, recv_sem):
        for p in peers:
            pltpu.make_async_remote_copy(
                src_ref=dst.at[h, :, p], dst_ref=dst.at[h, :, p],
                send_sem=send_sem.at[h, 0], recv_sem=recv_sem.at[h, p],
                device_id=(dp, p), device_id_type=MESH,
            ).wait_recv()

    def project(p):
        slot, c = turns[p]
        e, at_rows = stretch_of(c)
        wait_rest(p)
        sum_k[...] = jnp.zeros_like(sum_k)
        sum_v[...] = jnp.zeros_like(sum_v)

        @pl.loop(0, 2 * per)
        def _(i):
            j, at = lax.div(i, per), lax.rem(i, per)
            cols = pl.ds(pl.multiple_of(at * deep, deep), deep)
            rows = hid[slot, j, e, :, at_rows, cols].reshape(n_seq * piece_len, deep)
            sum_k[...] += jnp.dot(rows, key_all[i], preferred_element_type=f32)
            sum_v[...] += jnp.dot(rows, val_all[i], preferred_element_type=f32)

        shape = (n_seq, piece_len, HEAD_WIDTH)
        for kv in range(kv_heads):
            lanes = pl.ds(kv * HEAD_WIDTH, HEAD_WIDTH)
            raw_k[slot, kv, e, :, at_rows, :] = sum_k[:, lanes].reshape(shape)
            raw_v[slot, kv, e, :, at_rows, :] = sum_v[:, lanes].reshape(shape)
            raw_h[slot, kv, e, :, at_rows, :] = sum_v[:, lanes].reshape(shape).astype(bf16)
        if slot == 1:
            for kv in range(kv_heads):
                for copy in raw_copies(kv, c):
                    start(copy)

    def raw_copies(kv, c):
        e, at = stretch_of(c)
        return [
            pltpu.make_async_remote_copy(
                src_ref=src.at[1, kv, e, :, at], dst_ref=dst.at[kv, e, :, at],
                send_sem=send_sem.at[kv, c], recv_sem=recv_sem.at[kv, c],
                device_id=(twin, seq), device_id_type=MESH,
            )
            for src, dst, send_sem, recv_sem in (
                (raw_k, in_k, k_send, k_recv), (raw_h, in_v, v_send, v_recv),
            )
        ]

    def settle(kv):
        lanes = pl.ds(kv * HEAD_WIDTH, HEAD_WIDTH)
        for c in range(4):
            for copy in raw_copies(kv, c):
                copy.wait_recv()
        flat = (total, HEAD_WIDTH)
        raw = raw_k[0, kv].reshape(flat) + in_k[kv].reshape(flat)
        swapped = jnp.concatenate([raw[:, half:], raw[:, :half]], axis=1)
        keys[:, lanes] = (raw * cos[...] + swapped * sin[...]).astype(bf16)
        vals[:, lanes] = (raw_v[0, kv].reshape(flat) + in_v[kv].reshape(flat).astype(f32)).astype(bf16)

    scale = 1.0 / math.sqrt(HEAD_WIDTH)
    nt = (((1,), (1,)), ((), ()))
    tn = (((0,), (0,)), ((), ()))

    pack = 2 if group % 2 == 0 else 1
    half_seq = n_seq // 2
    rows_n = half_seq * tokens
    tri_shape = (pack * rows_n, rows_n)
    tri_row = lax.rem(lax.broadcasted_iota(jnp.int32, tri_shape, 0), rows_n)
    tri = lax.broadcasted_iota(jnp.int32, tri_shape, 1) <= tri_row

    def attend(kv):
        lanes = pl.ds(kv * HEAD_WIDTH, HEAD_WIDTH)
        key_acc[...] = jnp.zeros_like(key_acc)
        val_acc[...] = jnp.zeros_like(val_acc)

        @pl.loop(0, group // pack)
        def _(m):
            first = kv * group + m * pack
            for n in range(pack):
                h = first + n
                wait_exchange(h, qry, qry_send, qry_recv)
                wait_exchange(h, grd, grd_send, grd_recv)
                for copy in own_loads(h):
                    pltpu.make_async_copy(*copy).wait()
            for b in range(4):
                span, seqs = (b + 1) * rows_n, pl.ds(b % 2 * half_seq, half_seq)
                flat = (pack * rows_n, HEAD_WIDTH)
                q = qry[pl.ds(first, pack), b // 2, seqs].reshape(flat)
                g = grd[pl.ds(first, pack), b // 2, seqs].reshape(flat)
                k, v = keys[:span, lanes], vals[:span, lanes]
                s = lax.dot_general(q, k, nt, preferred_element_type=f32) * scale
                last = jnp.where(tri, s[:, span - rows_n:], -jnp.inf)
                s = last if b == 0 else jnp.concatenate([s[:, :span - rows_n], last], axis=1)
                e = jnp.exp(s - jnp.max(s, axis=1, keepdims=True))
                p = e * (1.0 / jnp.sum(e, axis=1, keepdims=True))
                p_half = p.astype(bf16)
                o = jnp.dot(p_half, v, preferred_element_type=f32).astype(bf16)
                dot = jnp.sum(g.astype(f32) * o.astype(f32), axis=1, keepdims=True)
                gp = lax.dot_general(g, v, nt, preferred_element_type=f32)
                ds = (p * (gp - dot) * scale).astype(bf16)
                dq = jnp.dot(ds, k, preferred_element_type=f32).astype(bf16)
                for n in range(pack):
                    start_n = pl.multiple_of((m * pack + n) * HEAD_WIDTH, HEAD_WIDTH)
                    head = pl.ds(start_n, HEAD_WIDTH)
                    shape = (half_seq, tokens, HEAD_WIDTH)
                    rows = slice(n * rows_n, (n + 1) * rows_n)
                    attn[kv, b // 2, seqs, :, head] = o[rows].reshape(shape)
                    qgrad[kv, b // 2, seqs, :, head] = dq[rows].reshape(shape)
                key_acc[:, :span] += lax.dot_general(q, ds, tn, preferred_element_type=f32)
                val_acc[:, :span] += lax.dot_general(g, p_half, tn, preferred_element_type=f32)

        grown = key_acc[...]
        swapped = jnp.concatenate([grown[half:, :], grown[:half, :]], axis=0)
        pre_t[kv, :HEAD_WIDTH, :] = (grown * cos_t[...] - swapped * sin_t[...]).astype(bf16)
        pre_t[kv, HEAD_WIDTH:, :] = val_acc[...].astype(bf16)

    def pre_copy(kv):
        return pltpu.make_async_remote_copy(
            src_ref=pre_t.at[kv], dst_ref=pre_in.at[kv],
            send_sem=pre_send.at[kv], recv_sem=pre_recv.at[kv],
            device_id=(twin, seq), device_id_type=MESH,
        )

    height, depth = acc.shape[3], deep
    results = ((attn, attn_out, a_send, a_recv), (qgrad, qgrad_out, q_send, q_recv))

    def own_store(kv, which):
        src, dst, _, _ = results[which]
        return pltpu.make_async_copy(
            src.at[kv, :, seq], dst.at[:, :, head_cols(seq, kv)], store_sem.at[which, kv]
        )

    def give_back(kv):
        for which, (src, dst, send_sem, recv_sem) in enumerate(results):
            for i, p in enumerate(peers):
                start(pltpu.make_async_remote_copy(
                    src_ref=src.at[kv, :, p], dst_ref=dst.at[:, :, head_cols(seq, kv)],
                    send_sem=send_sem.at[kv, i], recv_sem=recv_sem.at[kv, seq],
                    device_id=(dp, p), device_id_type=MESH,
                ))
            own_store(kv, which).start()

    def wait_back(kv):
        for which, (src, dst, send_sem, recv_sem) in enumerate(results):
            for p in peers:
                pltpu.make_async_remote_copy(
                    src_ref=src.at[kv, :, p], dst_ref=dst.at[:, :, head_cols(p, kv)],
                    send_sem=send_sem.at[kv, 0], recv_sem=recv_sem.at[kv, p],
                    device_id=(dp, p), device_id_type=MESH,
                ).wait_recv()
            own_store(kv, which).wait()

    parts = depth // tile

    def mate_copy(kv, w, t):
        return pltpu.make_async_remote_copy(
            src_ref=mate_out.at[kv, w, t], dst_ref=mate_in.at[kv, w, t],
            send_sem=mate_send.at[kv, w, t], recv_sem=mate_recv.at[kv, w, t],
            device_id=(mate, seq), device_id_type=MESH,
        )

    def far_copy(kv, i, w, t, back=False):
        at = w if back else slot_w
        return pltpu.make_async_remote_copy(
            src_ref=far_out.at[kv, i, t], dst_ref=far_in.at[kv, at, t],
            send_sem=far_send.at[kv, i, t], recv_sem=far_recv.at[kv, at, t],
            device_id=(owner(w), seq), device_id_type=MESH,
        )

    def part_of(pre, kv, slot, piece, t):
        j, at = lax.div(piece, per), lax.rem(piece, per)
        cols = pl.ds(pl.multiple_of(at * depth + t * tile, tile), tile)
        rows = hid[slot, j, :, :, :, cols].reshape(total, tile)
        return jnp.dot(pre[kv], rows, preferred_element_type=f32)

    def own_products(kv):
        for w in others + [slot_w]:
            @pl.loop(0, parts)
            def _(t):
                mate_acc[kv, w, t] = part_of(pre_t, kv, 0, w * CORES + 1 - core, t)
                acc[kv, w, t] = part_of(pre_t, kv, 0, w * CORES + core, t)

    def twin_products(kv):
        def to_mate(w):
            @pl.loop(0, parts)
            def _(t):
                v = mate_acc[kv, w, t] + part_of(pre_in, kv, 1, w * CORES + 1 - core, t)
                mate_out[kv, w, t] = v.astype(bf16)
                mate_copy(kv, w, t).start()

        def to_acc(w):
            @pl.loop(0, parts)
            def _(t):
                acc[kv, w, t] += part_of(pre_in, kv, 1, w * CORES + core, t)

        pre_copy(kv).wait_recv()
        for w in others:
            to_mate(w)
        for w in others:
            to_acc(w)
        for i, w in enumerate(others):
            @pl.loop(0, parts)
            def _(t):
                mate_copy(kv, w, t).wait_recv()
                v = acc[kv, w, t] + mate_in[kv, w, t].astype(f32)
                far_out[kv, i, t] = v.astype(bf16)
                far_copy(kv, i, w, t).start()
        to_mate(slot_w)
        to_acc(slot_w)

        @pl.loop(0, parts)
        def _(t):
            mate_copy(kv, slot_w, t).wait_recv()
            acc[kv, slot_w, t] += mate_in[kv, slot_w, t].astype(f32)

    def finish(kv):
        lanes = pl.ds(kv * HEAD_WIDTH, HEAD_WIDTH)
        for t in range(parts):
            v = acc[kv, slot_w, t]
            for i, w in enumerate(others):
                far_copy(kv, i, w, t, True).wait_recv()
                v = v + far_in[kv, w, t].astype(f32)
            at = pl.ds(t * tile, tile)
            key_grad[at, lanes] = v[:HEAD_WIDTH, :].T
            val_grad[at, lanes] = v[HEAD_WIDTH:, :].T

    for c in range(4):
        e, at = stretch_of(c)
        for j in range(2):
            src = hidden.at[e, at, embed_cols(1 - side, j)]
            start(hidden_copy(1, c, j, seq, twin, seq, hid_send.at[next(slots)], src))
            for i, w in enumerate(others):
                start(far_weight(c // 2, c % 2 * 2 + j, i, w, slot_w))
    for kind in range(2):
        start(weight_copy(kind, mine, mate, mate_w_send.at[0, kind], True))
    for copy in loads:
        pltpu.make_async_copy(*copy).start()
    direct(0)
    for h in range(kv_heads * group):
        for copy in own_loads(h):
            pltpu.make_async_copy(*copy).start()
    for p in range(5):
        direct(p + 1)
        relay_hidden(p)
    direct(6)
    relay_hidden(5)
    direct(7)
    relay_weights()
    for copy in loads:
        pltpu.make_async_copy(*copy).wait()
    wait_weights()
    project(2)
    project(4)
    relay_hidden(6)
    project(5)
    relay_hidden(7)
    for h in range(kv_heads * group):
        exchange(h, queries, qry, qry_send, qry_recv)
        exchange(h, out_grad, grd, grd_send, grd_recv)
    for p in (6, 0, 1, 3, 7):
        project(p)
    for kv in range(kv_heads):
        settle(kv)
        attend(kv)
        start(pre_copy(kv))
        if kv > 0:
            twin_products(kv - 1)
            give_back(kv - 1)
        own_products(kv)
    give_back(kv_heads - 1)
    twin_products(kv_heads - 1)
    for kv in range(kv_heads):
        finish(kv)
        wait_back(kv)
    for kv in range(kv_heads):
        for t in range(parts):
            for w in range(near):
                mate_copy(kv, w, t).wait_send()
            for i, w in enumerate(others):
                far_copy(kv, i, w, t).wait_send()
    for copy in sends:
        copy.wait_send()


def put_kernel(*refs):
    count = len(refs) // 2
    sem = refs[-1]
    copies = [
        pltpu.make_async_copy(refs[i], refs[count + i], sem.at[i]) for i in range(count)
    ]
    for copy in copies:
        copy.start()
    for copy in copies:
        copy.wait()


def put_all(*arrays):
    return pl.pallas_call(
        put_kernel,
        out_shape=[jax.ShapeDtypeStruct(x.shape, x.dtype) for x in arrays],
        in_specs=[pl.BlockSpec(memory_space=pltpu.VMEM)] * len(arrays),
        out_specs=[ANY] * len(arrays),
        scratch_shapes=[pltpu.SemaphoreType.DMA((len(arrays),))],
        compiler_params=pltpu.CompilerParams(vmem_limit_bytes=1 << 20),
        name="put_all",
    )(*arrays)


def local(n_seq, n_dp, hidden, queries, key_matrix, value_matrix, out_grad):
    _, stretches, tokens, embed = hidden.shape
    full = queries.shape[3]
    width = full // n_seq
    deep, kv_width = key_matrix.shape
    kv_heads = kv_width // HEAD_WIDTH
    group = width // kv_width
    wide = group * HEAD_WIDTH
    near = n_dp // CORES // 2
    quarter = embed // 4
    rows, cols = grid_of(n_seq)
    hid_sends = 8 * (2 * (rows - 1 + cols - 1) + 2 * (rows - 1) * (cols - 1)) + 8
    total = stretches * n_seq * tokens
    block = n_seq * tokens
    bf16, f32 = jnp.bfloat16, jnp.float32
    dma = pltpu.SemaphoreType.DMA
    half = HEAD_WIDTH // 2
    inverse = np.exp(
        np.arange(half, dtype=np.float32) * np.float32(-2.0 * math.log(ROPE_BASE) / HEAD_WIDTH)
    ).astype(np.float32)
    phase = np.arange(total, dtype=np.float32)[:, None] * inverse[None, :]
    cos_half, sin_half = np.cos(phase), np.sin(phase)
    cos = np.concatenate([cos_half, cos_half], axis=1).astype(np.float32)
    sin = np.concatenate([-sin_half, sin_half], axis=1).astype(np.float32)
    heads = (kv_heads, stretches, n_seq, tokens, wide)
    single = (kv_heads * group, stretches, n_seq, tokens, HEAD_WIDTH)
    height = 2 * HEAD_WIDTH
    tile = math.gcd(deep, 256)
    parts = deep // tile
    blocks = (kv_heads, near, parts, height, tile)
    weights = (n_dp // 2, deep, kv_width)
    raw = (kv_heads, stretches, n_seq, tokens, HEAD_WIDTH)
    all_heads = kv_heads * group
    spare = max(near - 1, 1)
    attn_out, query_grad, key_grad, val_grad = pl.pallas_call(
        functools.partial(kernel, n_seq, n_dp, kv_heads, group, tile),
        out_shape=[
            pltpu.VMEM((stretches, tokens, full), bf16),
            pltpu.VMEM((stretches, tokens, full), bf16),
            pltpu.VMEM((deep, kv_width), f32),
            pltpu.VMEM((deep, kv_width), f32),
        ],
        in_specs=[ANY] * 5 + [VMEM] * 4,
        out_specs=[VMEM] * 4,
        scratch_shapes=[
            pltpu.VMEM((2, 2, stretches, n_seq, tokens, quarter), bf16),
            pltpu.VMEM(single, bf16),
            pltpu.VMEM(single, bf16),
            pltpu.VMEM(weights, bf16),
            pltpu.VMEM(weights, bf16),
            pltpu.VMEM((block // 2, kv_width), f32),
            pltpu.VMEM((block // 2, kv_width), f32),
            pltpu.VMEM((2,) + raw, f32),
            pltpu.VMEM((2,) + raw, f32),
            pltpu.VMEM((2,) + raw, bf16),
            pltpu.VMEM(raw, f32),
            pltpu.VMEM(raw, bf16),
            pltpu.VMEM((total, kv_width), bf16),
            pltpu.VMEM((total, kv_width), bf16),
            pltpu.VMEM(heads, bf16),
            pltpu.VMEM(heads, bf16),
            pltpu.VMEM((kv_heads, height, total), bf16),
            pltpu.VMEM((kv_heads, height, total), bf16),
            pltpu.VMEM((HEAD_WIDTH, total), f32),
            pltpu.VMEM((HEAD_WIDTH, total), f32),
            pltpu.VMEM(blocks, f32),
            pltpu.VMEM(blocks, f32),
            pltpu.VMEM(blocks, bf16),
            pltpu.VMEM(blocks, bf16),
            pltpu.VMEM((kv_heads, spare, parts, height, tile), bf16),
            pltpu.VMEM(blocks, bf16),
            dma((2,)), dma((2, all_heads)), dma((2, kv_heads)),
            dma((hid_sends,)), dma((2, 4, 2, n_seq)),
            dma((all_heads, n_seq)), dma((all_heads, n_seq)),
            dma((all_heads, n_seq)), dma((all_heads, n_seq)),
            dma((spare, 2, 4)), dma((near, 2, 4)), dma((near, 2)), dma((n_dp // 2, 2)),
            dma((kv_heads, 4)), dma((kv_heads, 4)),
            dma((kv_heads, 4)), dma((kv_heads, 4)),
            dma((kv_heads,)), dma((kv_heads,)),
            dma((kv_heads, n_seq)), dma((kv_heads, n_seq)),
            dma((kv_heads, n_seq)), dma((kv_heads, n_seq)),
            dma((kv_heads, near, parts)), dma((kv_heads, near, parts)),
            dma((kv_heads, spare, parts)), dma((kv_heads, near, parts)),
        ],
        compiler_params=pltpu.CompilerParams(
            collective_id=0, has_side_effects=True, vmem_limit_bytes=VMEM_LIMIT
        ),
        name="attention_step",
    )(hidden[0], queries[0], key_matrix, value_matrix, out_grad[0],
      cos, sin, cos.T.copy(), sin.T.copy())
    attn_out, query_grad, key_grad, val_grad = put_all(
        attn_out, query_grad, key_grad, val_grad
    )
    return attn_out[None], query_grad[None], key_grad, val_grad


def solution(mesh):
    n_dp, n_seq = mesh.shape["dp"], mesh.shape["seq"]
    tokens, weights = P("dp", None, "seq", None), P("dp", "seq")
    return jax.shard_map(
        functools.partial(local, n_seq, n_dp),
        mesh=mesh,
        in_specs=(tokens, tokens, weights, weights, tokens),
        out_specs=(tokens, tokens, weights, weights),
        check_vma=False,
    )
```

```python
import functools
import math

import jax
import jax.numpy as jnp
import numpy as np
from jax import lax
from jax.experimental import pallas as pl
from jax.experimental.pallas import tpu as pltpu
from jax.sharding import PartitionSpec as P

HEAD_WIDTH = 128
ROPE_BASE = 500000.0
CORES = 2
MESH = pl.DeviceIdType.MESH
ANY = pl.BlockSpec(memory_space=pl.ANY)
VMEM = pl.BlockSpec(memory_space=pltpu.VMEM)
VMEM_LIMIT = 56 << 20
TILE = 1024


def grid_of(count):
    rows = 2 if count % 2 == 0 else 1
    return rows, count // rows


def place(n_seq, n_dp):
    dp, seq = lax.axis_index("dp"), lax.axis_index("seq")
    chips = n_dp // CORES
    chip, core = lax.div(dp, CORES), lax.rem(dp, CORES)
    rows, cols = grid_of(n_seq)
    row, col = lax.div(seq, cols), lax.rem(seq, cols)
    row_peers = [row * cols + lax.rem(col + d, cols) for d in range(1, cols)]
    col_peers = [lax.rem(row + d, rows) * cols + col for d in range(1, rows)]
    far_peers = [
        lax.rem(row + e, rows) * cols + lax.rem(col + d, cols)
        for e in range(1, rows)
        for d in range(1, cols)
    ]
    return dp, seq, chips, chip, core, row_peers, col_peers, far_peers


def kernel(
    n_seq, n_dp, kv_heads, group, tile,
    hidden, queries, key_matrix, value_matrix, out_grad, cos, sin, cos_t, sin_t,
    attn_out, qgrad_out, key_grad, val_grad,
    hid, qry, grd, key_all, val_all, sum_k, sum_v, raw_k, raw_v, raw_h, in_k, in_v,
    keys, vals, attn, qgrad, pre_t, pre_in,
    key_acc, val_acc, acc, mate_acc, mate_out, mate_in, far_out, far_in,
    load_sem, own_sem, store_sem, hid_send, hid_recv, qry_send, qry_recv, grd_send, grd_recv,
    far_w_send, far_w_recv, mate_w_send, w_recv, k_send, k_recv, v_send, v_recv, pre_send, pre_recv,
    a_send, a_recv, q_send, q_recv, mate_send, mate_recv, far_send, far_recv,
):
    f32, bf16 = jnp.float32, jnp.bfloat16
    dp, seq, chips, chip, core, row_peers, col_peers, far_peers = place(n_seq, n_dp)
    peers = row_peers + col_peers + far_peers
    near = chips // 2
    side, slot_w = lax.div(chip, near), lax.rem(chip, near)
    mate = chip * CORES + 1 - core
    twin = ((1 - side) * near + slot_w) * CORES + core
    others = [lax.rem(slot_w + d, near) for d in range(1, near)]

    def owner(w):
        return (side * near + w) * CORES + core

    wide = group * HEAD_WIDTH
    width = kv_heads * wide
    total = keys.shape[0]
    half = HEAD_WIDTH // 2
    block = total // 2
    deep = key_all.shape[1]
    quarter = hid.shape[-1]
    per = quarter // deep
    mine = slot_w * CORES + core
    tokens = hid.shape[4]
    piece_len = tokens // 2
    turns = ((0, 0), (0, 1), (1, 0), (0, 2), (1, 1), (1, 2), (1, 3), (0, 3))

    def stretch_of(c):
        return c // 2, pl.ds(c % 2 * piece_len, piece_len)

    barrier = pltpu.get_barrier_semaphore()
    greeted = [(dp, p) for p in peers] + [(mate, seq), (twin, seq)]
    greeted += [(owner(w), seq) for w in others]
    for device in greeted:
        pl.semaphore_signal(barrier, inc=1, device_id=device, device_id_type=MESH)
    pl.semaphore_wait(barrier, len(greeted))

    def head_cols(target, kv):
        return pl.ds(pl.multiple_of(target * width + kv * wide, wide), wide)

    def one_head(target, h):
        start = pl.multiple_of(target * width + h * HEAD_WIDTH, HEAD_WIDTH)
        return pl.ds(start, HEAD_WIDTH)

    def embed_cols(which, j):
        return pl.ds(pl.multiple_of((which * 2 + j) * quarter, quarter), quarter)

    loads = [
        (key_matrix, key_all.at[mine], load_sem.at[0]),
        (value_matrix, val_all.at[mine], load_sem.at[1]),
    ]
    for c in range(4):
        e, at = stretch_of(c)
        for j in range(2):
            pltpu.make_async_copy(
                hidden.at[e, at, embed_cols(side, j)], hid.at[0, j, e, seq, at],
                hid_recv.at[0, c, j, seq],
            ).start()

    def own_loads(h):
        return (
            (queries.at[:, :, one_head(seq, h)], qry.at[h, :, seq], own_sem.at[0, h]),
            (out_grad.at[:, :, one_head(seq, h)], grd.at[h, :, seq], own_sem.at[1, h]),
        )

    sends = []

    def start(copy):
        copy.start()
        sends.append(copy)

    slots = iter(range(hid_send.shape[0]))

    def hidden_copy(slot, c, j, source, target_dp, target, send_sem, src=None):
        e, at = stretch_of(c)
        dst = hid.at[slot, j, e, source, at]
        return pltpu.make_async_remote_copy(
            src_ref=dst if src is None else src, dst_ref=dst,
            send_sem=send_sem, recv_sem=hid_recv.at[slot, c, j, source],
            device_id=(target_dp, target), device_id_type=MESH,
        )

    def send_hidden(slot, c, j, source, target, src=None):
        start(hidden_copy(slot, c, j, source, dp, target, hid_send.at[next(slots)], src))

    def wait_hidden(slot, c, j, source):
        hidden_copy(slot, c, j, source, dp, source, hid_send.at[0]).wait_recv()

    def direct(p):
        slot, c = turns[p]
        e, at = stretch_of(c)
        if slot == 1:
            for j in range(2):
                wait_hidden(slot, c, j, seq)

        def source(j):
            return None if slot == 1 else hidden.at[e, at, embed_cols(side, j)]

        for j in range(2):
            for q in row_peers:
                send_hidden(slot, c, j, seq, q, source(j))
            for q in col_peers:
                send_hidden(slot, c, 1 - j, seq, q, source(1 - j))

    def relay_hidden(p):
        slot, c = turns[p]
        for r in row_peers:
            wait_hidden(slot, c, 0, r)
            for q in col_peers:
                send_hidden(slot, c, 0, r, q)
        for r in col_peers:
            wait_hidden(slot, c, 1, r)
            for q in row_peers:
                send_hidden(slot, c, 1, r, q)

    def wait_rest(p):
        slot, c = turns[p]
        for r in row_peers:
            wait_hidden(slot, c, 1, r)
        for r in col_peers:
            wait_hidden(slot, c, 0, r)
        for r in far_peers:
            wait_hidden(slot, c, 0, r)
            wait_hidden(slot, c, 1, r)

    tables = (key_all, val_all)
    owns = (key_matrix, value_matrix)

    def weight_copy(kind, piece, target_dp, send_sem, own=False):
        return pltpu.make_async_remote_copy(
            src_ref=owns[kind] if own else tables[kind].at[piece],
            dst_ref=tables[kind].at[piece],
            send_sem=send_sem, recv_sem=w_recv.at[piece, kind],
            device_id=(target_dp, seq), device_id_type=MESH,
        )

    strip = deep // 4

    def far_weight(kind, r, i, w, source):
        at = pl.ds(r * strip, strip)
        return pltpu.make_async_remote_copy(
            src_ref=owns[kind].at[at], dst_ref=tables[kind].at[source * CORES + core, at],
            send_sem=far_w_send.at[i, kind, r], recv_sem=far_w_recv.at[source, kind, r],
            device_id=(owner(w), seq), device_id_type=MESH,
        )

    def relay_weights(kind):
        for i, w in enumerate(others):
            for r in range(4):
                far_weight(kind, r, i, w, w).wait_recv()
            start(weight_copy(kind, w * CORES + core, mate, mate_w_send.at[i + 1, kind]))

    def wait_weights():
        for w in [slot_w] + others:
            for kind in range(2):
                piece = w * CORES + 1 - core
                weight_copy(kind, piece, mate, mate_w_send.at[0, kind]).wait_recv()

    def exchange(h, src, dst, send_sem, recv_sem):
        for i, p in enumerate(peers):
            start(pltpu.make_async_remote_copy(
                src_ref=src.at[:, :, one_head(p, h)], dst_ref=dst.at[h, :, seq],
                send_sem=send_sem.at[h, i], recv_sem=recv_sem.at[h, seq],
                device_id=(dp, p), device_id_type=MESH,
            ))

    def wait_exchange(h, dst, send_sem, recv_sem):
        for p in peers:
            pltpu.make_async_remote_copy(
                src_ref=dst.at[h, :, p], dst_ref=dst.at[h, :, p],
                send_sem=send_sem.at[h, 0], recv_sem=recv_sem.at[h, p],
                device_id=(dp, p), device_id_type=MESH,
            ).wait_recv()

    def project(p):
        slot, c = turns[p]
        e, at_rows = stretch_of(c)
        wait_rest(p)
        if slot == 0:
            for j in range(2):
                wait_hidden(slot, c, j, seq)
        sum_k[...] = jnp.zeros_like(sum_k)
        sum_v[...] = jnp.zeros_like(sum_v)

        @pl.loop(0, 2 * per)
        def _(i):
            j, at = lax.div(i, per), lax.rem(i, per)
            cols = pl.ds(pl.multiple_of(at * deep, deep), deep)
            rows = hid[slot, j, e, :, at_rows, cols].reshape(n_seq * piece_len, deep)
            sum_k[...] += jnp.dot(rows, key_all[i], preferred_element_type=f32)
            sum_v[...] += jnp.dot(rows, val_all[i], preferred_element_type=f32)

        shape = (n_seq, piece_len, HEAD_WIDTH)
        for kv in range(kv_heads):
            lanes = pl.ds(kv * HEAD_WIDTH, HEAD_WIDTH)
            raw_k[slot, kv, e, :, at_rows, :] = sum_k[:, lanes].reshape(shape)
            raw_v[slot, kv, e, :, at_rows, :] = sum_v[:, lanes].reshape(shape)
            raw_h[slot, kv, e, :, at_rows, :] = sum_v[:, lanes].reshape(shape).astype(bf16)
        if slot == 1:
            for kv in range(kv_heads):
                for copy in raw_copies(kv, c):
                    start(copy)

    def raw_copies(kv, c):
        e, at = stretch_of(c)
        return [
            pltpu.make_async_remote_copy(
                src_ref=src.at[1, kv, e, :, at], dst_ref=dst.at[kv, e, :, at],
                send_sem=send_sem.at[kv, c], recv_sem=recv_sem.at[kv, c],
                device_id=(twin, seq), device_id_type=MESH,
            )
            for src, dst, send_sem, recv_sem in (
                (raw_k, in_k, k_send, k_recv), (raw_h, in_v, v_send, v_recv),
            )
        ]

    def settle(kv):
        lanes = pl.ds(kv * HEAD_WIDTH, HEAD_WIDTH)
        for c in range(4):
            for copy in raw_copies(kv, c):
                copy.wait_recv()
        flat = (total, HEAD_WIDTH)
        raw = raw_k[0, kv].reshape(flat) + in_k[kv].reshape(flat)
        swapped = jnp.concatenate([raw[:, half:], raw[:, :half]], axis=1)
        keys[:, lanes] = (raw * cos[...] + swapped * sin[...]).astype(bf16)
        vals[:, lanes] = (raw_v[0, kv].reshape(flat) + in_v[kv].reshape(flat).astype(f32)).astype(bf16)

    scale = 1.0 / math.sqrt(HEAD_WIDTH)
    nt = (((1,), (1,)), ((), ()))
    tn = (((0,), (0,)), ((), ()))

    pack = 2 if group % 2 == 0 else 1
    half_seq = n_seq // 2
    rows_n = half_seq * tokens
    tri_shape = (pack * rows_n, rows_n)
    tri_row = lax.rem(lax.broadcasted_iota(jnp.int32, tri_shape, 0), rows_n)
    tri = lax.broadcasted_iota(jnp.int32, tri_shape, 1) <= tri_row

    def attend(kv, between=None):
        lanes = pl.ds(kv * HEAD_WIDTH, HEAD_WIDTH)
        key_acc[...] = jnp.zeros_like(key_acc)
        val_acc[...] = jnp.zeros_like(val_acc)

        @pl.loop(0, group // pack)
        def _(m):
            first = kv * group + m * pack
            if between is not None:
                pl.when(m == group // pack - 1)(between)
            for n in range(pack):
                h = first + n
                wait_exchange(h, qry, qry_send, qry_recv)
                wait_exchange(h, grd, grd_send, grd_recv)
                for copy in own_loads(h):
                    pltpu.make_async_copy(*copy).wait()
            for b in range(4):
                span, seqs = (b + 1) * rows_n, pl.ds(b % 2 * half_seq, half_seq)
                flat = (pack * rows_n, HEAD_WIDTH)
                q = qry[pl.ds(first, pack), b // 2, seqs].reshape(flat)
                g = grd[pl.ds(first, pack), b // 2, seqs].reshape(flat)
                k, v = keys[:span, lanes], vals[:span, lanes]
                s = lax.dot_general(q, k, nt, preferred_element_type=f32) * scale
                last = jnp.where(tri, s[:, span - rows_n:], -jnp.inf)
                s = last if b == 0 else jnp.concatenate([s[:, :span - rows_n], last], axis=1)
                e = jnp.exp(s - jnp.max(s, axis=1, keepdims=True))
                p = e * (1.0 / jnp.sum(e, axis=1, keepdims=True))
                p_half = p.astype(bf16)
                o = jnp.dot(p_half, v, preferred_element_type=f32).astype(bf16)
                dot = jnp.sum(g.astype(f32) * o.astype(f32), axis=1, keepdims=True)
                gp = lax.dot_general(g, v, nt, preferred_element_type=f32)
                ds = (p * (gp - dot) * scale).astype(bf16)
                dq = jnp.dot(ds, k, preferred_element_type=f32).astype(bf16)
                for n in range(pack):
                    start_n = pl.multiple_of((m * pack + n) * HEAD_WIDTH, HEAD_WIDTH)
                    head = pl.ds(start_n, HEAD_WIDTH)
                    shape = (half_seq, tokens, HEAD_WIDTH)
                    rows = slice(n * rows_n, (n + 1) * rows_n)
                    attn[kv, b // 2, seqs, :, head] = o[rows].reshape(shape)
                    qgrad[kv, b // 2, seqs, :, head] = dq[rows].reshape(shape)
                key_acc[:, :span] += lax.dot_general(q, ds, tn, preferred_element_type=f32)
                val_acc[:, :span] += lax.dot_general(g, p_half, tn, preferred_element_type=f32)

        grown = key_acc[...]
        swapped = jnp.concatenate([grown[half:, :], grown[:half, :]], axis=0)
        pre_t[kv, 0] = (grown * cos_t[...] - swapped * sin_t[...]).astype(bf16)
        pre_t[kv, 1] = val_acc[...].astype(bf16)

    def pre_copy(kv, u):
        return pltpu.make_async_remote_copy(
            src_ref=pre_t.at[kv, u], dst_ref=pre_in.at[kv, u],
            send_sem=pre_send.at[kv, u], recv_sem=pre_recv.at[kv, u],
            device_id=(twin, seq), device_id_type=MESH,
        )

    depth = deep
    results = ((attn, attn_out, a_send, a_recv), (qgrad, qgrad_out, q_send, q_recv))

    def own_store(kv, which):
        src, dst, _, _ = results[which]
        return pltpu.make_async_copy(
            src.at[kv, :, seq], dst.at[:, :, head_cols(seq, kv)], store_sem.at[which, kv]
        )

    def give_back(kv):
        for which, (src, dst, send_sem, recv_sem) in enumerate(results):
            for i, p in enumerate(peers):
                start(pltpu.make_async_remote_copy(
                    src_ref=src.at[kv, :, p], dst_ref=dst.at[:, :, head_cols(seq, kv)],
                    send_sem=send_sem.at[kv, i], recv_sem=recv_sem.at[kv, seq],
                    device_id=(dp, p), device_id_type=MESH,
                ))
            own_store(kv, which).start()

    def wait_back(kv):
        for which, (src, dst, send_sem, recv_sem) in enumerate(results):
            for p in peers:
                pltpu.make_async_remote_copy(
                    src_ref=src.at[kv, :, p], dst_ref=dst.at[:, :, head_cols(p, kv)],
                    send_sem=send_sem.at[kv, 0], recv_sem=recv_sem.at[kv, p],
                    device_id=(dp, p), device_id_type=MESH,
                ).wait_recv()
            own_store(kv, which).wait()

    parts = depth // tile

    def mate_copy(kv, w, u, t):
        return pltpu.make_async_remote_copy(
            src_ref=mate_out.at[kv, w, u, t], dst_ref=mate_in.at[kv, w, u, t],
            send_sem=mate_send.at[kv, w, u, t], recv_sem=mate_recv.at[kv, w, u, t],
            device_id=(mate, seq), device_id_type=MESH,
        )

    def far_copy(kv, i, w, u, t, back=False):
        at = w if back else slot_w
        return pltpu.make_async_remote_copy(
            src_ref=far_out.at[kv, i, u, t], dst_ref=far_in.at[kv, at, u, t],
            send_sem=far_send.at[kv, i, u, t], recv_sem=far_recv.at[kv, at, u, t],
            device_id=(owner(w), seq), device_id_type=MESH,
        )

    def part_of(left, slot, piece, t):
        j, at = lax.div(piece, per), lax.rem(piece, per)
        cols = pl.ds(pl.multiple_of(at * depth + t * tile, tile), tile)
        rows = hid[slot, j, :, :, :, cols].reshape(total, tile)
        return jnp.dot(left, rows, preferred_element_type=f32)

    def own_products(kv):
        left = pre_t.at[kv]

        def both(piece, t):
            return part_of(left[...].reshape(2 * HEAD_WIDTH, total), 0, piece, t)

        for w in others + [slot_w]:
            @pl.loop(0, parts)
            def _(t):
                out = both(w * CORES + 1 - core, t)
                mate_acc[kv, w, 0, t] = out[:HEAD_WIDTH]
                mate_acc[kv, w, 1, t] = out[HEAD_WIDTH:]
                out = both(w * CORES + core, t)
                acc[kv, w, 0, t] = out[:HEAD_WIDTH]
                acc[kv, w, 1, t] = out[HEAD_WIDTH:]

    def twin_products(kv, u):
        def to_mate(w):
            @pl.loop(0, parts)
            def _(t):
                v = mate_acc[kv, w, u, t] + part_of(pre_in[kv, u], 1, w * CORES + 1 - core, t)
                mate_out[kv, w, u, t] = v.astype(bf16)
                mate_copy(kv, w, u, t).start()

        def to_acc(w):
            @pl.loop(0, parts)
            def _(t):
                acc[kv, w, u, t] += part_of(pre_in[kv, u], 1, w * CORES + core, t)

        pre_copy(kv, u).wait_recv()
        for w in others:
            to_mate(w)
        for w in others:
            to_acc(w)
        for i, w in enumerate(others):
            @pl.loop(0, parts)
            def _(t):
                mate_copy(kv, w, u, t).wait_recv()
                v = acc[kv, w, u, t] + mate_in[kv, w, u, t].astype(f32)
                far_out[kv, i, u, t] = v.astype(bf16)
                far_copy(kv, i, w, u, t).start()
        to_mate(slot_w)
        to_acc(slot_w)

    def finish(kv, u):
        lanes = pl.ds(kv * HEAD_WIDTH, HEAD_WIDTH)
        grad = val_grad if u else key_grad
        for t in range(parts):
            mate_copy(kv, slot_w, u, t).wait_recv()
            v = acc[kv, slot_w, u, t] + mate_in[kv, slot_w, u, t].astype(f32)
            for i, w in enumerate(others):
                far_copy(kv, i, w, u, t, True).wait_recv()
                v = v + far_in[kv, w, u, t].astype(f32)
            grad[pl.ds(t * tile, tile), lanes] = v.T

    for c in range(4):
        e, at = stretch_of(c)
        for j in range(2):
            src = hidden.at[e, at, embed_cols(1 - side, j)]
            start(hidden_copy(1, c, j, seq, twin, seq, hid_send.at[next(slots)], src))
            for i, w in enumerate(others):
                start(far_weight(c // 2, c % 2 * 2 + j, i, w, slot_w))
    for kind in range(2):
        start(weight_copy(kind, mine, mate, mate_w_send.at[0, kind], True))
    for copy in loads:
        pltpu.make_async_copy(*copy).start()
    direct(0)
    for h in range(kv_heads * group):
        for copy in own_loads(h):
            pltpu.make_async_copy(*copy).start()
    for p in range(5):
        direct(p + 1)
        relay_hidden(p)
        if p == 4:
            relay_weights(0)
    direct(6)
    relay_hidden(5)
    direct(7)
    relay_weights(1)
    for copy in loads:
        pltpu.make_async_copy(*copy).wait()
    wait_weights()
    project(2)
    project(4)
    relay_hidden(6)
    project(5)
    relay_hidden(7)
    for h in range(kv_heads * group):
        exchange(h, queries, qry, qry_send, qry_recv)
        exchange(h, out_grad, grd, grd_send, grd_recv)
    for p in (6, 0, 1, 3, 7):
        project(p)
    for kv in range(kv_heads):
        settle(kv)
        attend(kv, functools.partial(twin_products, kv - 1, 1) if kv else None)
        for u in (1, 0):
            start(pre_copy(kv, u))
        if kv:
            twin_products(kv - 1, 0)
        own_products(kv)
        give_back(kv)
    for u in (1, 0):
        twin_products(kv_heads - 1, u)
    for kv in range(kv_heads):
        for u in (1, 0):
            finish(kv, u)
        wait_back(kv)
    for kv in range(kv_heads):
        for u in range(2):
            for t in range(parts):
                for w in range(near):
                    mate_copy(kv, w, u, t).wait_send()
                for i, w in enumerate(others):
                    far_copy(kv, i, w, u, t).wait_send()
    for copy in sends:
        copy.wait_send()


def put_kernel(*refs):
    count = len(refs) // 2
    sem = refs[-1]
    copies = [
        pltpu.make_async_copy(refs[i], refs[count + i], sem.at[i]) for i in range(count)
    ]
    for copy in copies:
        copy.start()
    for copy in copies:
        copy.wait()


def put_all(*arrays):
    return pl.pallas_call(
        put_kernel,
        out_shape=[jax.ShapeDtypeStruct(x.shape, x.dtype) for x in arrays],
        in_specs=[pl.BlockSpec(memory_space=pltpu.VMEM)] * len(arrays),
        out_specs=[ANY] * len(arrays),
        scratch_shapes=[pltpu.SemaphoreType.DMA((len(arrays),))],
        compiler_params=pltpu.CompilerParams(vmem_limit_bytes=1 << 20),
        name="put_all",
    )(*arrays)


def local(n_seq, n_dp, hidden, queries, key_matrix, value_matrix, out_grad):
    _, stretches, tokens, embed = hidden.shape
    full = queries.shape[3]
    width = full // n_seq
    deep, kv_width = key_matrix.shape
    kv_heads = kv_width // HEAD_WIDTH
    group = width // kv_width
    wide = group * HEAD_WIDTH
    near = n_dp // CORES // 2
    quarter = embed // 4
    rows, cols = grid_of(n_seq)
    hid_sends = 8 * (2 * (rows - 1 + cols - 1) + 2 * (rows - 1) * (cols - 1)) + 8
    total = stretches * n_seq * tokens
    block = n_seq * tokens
    bf16, f32 = jnp.bfloat16, jnp.float32
    dma = pltpu.SemaphoreType.DMA
    half = HEAD_WIDTH // 2
    inverse = np.exp(
        np.arange(half, dtype=np.float32) * np.float32(-2.0 * math.log(ROPE_BASE) / HEAD_WIDTH)
    ).astype(np.float32)
    phase = np.arange(total, dtype=np.float32)[:, None] * inverse[None, :]
    cos_half, sin_half = np.cos(phase), np.sin(phase)
    cos = np.concatenate([cos_half, cos_half], axis=1).astype(np.float32)
    sin = np.concatenate([-sin_half, sin_half], axis=1).astype(np.float32)
    heads = (kv_heads, stretches, n_seq, tokens, wide)
    single = (kv_heads * group, stretches, n_seq, tokens, HEAD_WIDTH)
    tile = math.gcd(deep, TILE)
    parts = deep // tile
    blocks = (kv_heads, near, 2, parts, HEAD_WIDTH, tile)
    weights = (n_dp // 2, deep, kv_width)
    raw = (kv_heads, stretches, n_seq, tokens, HEAD_WIDTH)
    all_heads = kv_heads * group
    spare = max(near - 1, 1)
    attn_out, query_grad, key_grad, val_grad = pl.pallas_call(
        functools.partial(kernel, n_seq, n_dp, kv_heads, group, tile),
        out_shape=[
            pltpu.VMEM((stretches, tokens, full), bf16),
            pltpu.VMEM((stretches, tokens, full), bf16),
            pltpu.VMEM((deep, kv_width), f32),
            pltpu.VMEM((deep, kv_width), f32),
        ],
        in_specs=[ANY] * 5 + [VMEM] * 4,
        out_specs=[VMEM] * 4,
        scratch_shapes=[
            pltpu.VMEM((2, 2, stretches, n_seq, tokens, quarter), bf16),
            pltpu.VMEM(single, bf16),
            pltpu.VMEM(single, bf16),
            pltpu.VMEM(weights, bf16),
            pltpu.VMEM(weights, bf16),
            pltpu.VMEM((block // 2, kv_width), f32),
            pltpu.VMEM((block // 2, kv_width), f32),
            pltpu.VMEM((2,) + raw, f32),
            pltpu.VMEM((2,) + raw, f32),
            pltpu.VMEM((2,) + raw, bf16),
            pltpu.VMEM(raw, f32),
            pltpu.VMEM(raw, bf16),
            pltpu.VMEM((total, kv_width), bf16),
            pltpu.VMEM((total, kv_width), bf16),
            pltpu.VMEM(heads, bf16),
            pltpu.VMEM(heads, bf16),
            pltpu.VMEM((kv_heads, 2, HEAD_WIDTH, total), bf16),
            pltpu.VMEM((kv_heads, 2, HEAD_WIDTH, total), bf16),
            pltpu.VMEM((HEAD_WIDTH, total), f32),
            pltpu.VMEM((HEAD_WIDTH, total), f32),
            pltpu.VMEM(blocks, f32),
            pltpu.VMEM(blocks, f32),
            pltpu.VMEM(blocks, bf16),
            pltpu.VMEM(blocks, bf16),
            pltpu.VMEM((kv_heads, spare, 2, parts, HEAD_WIDTH, tile), bf16),
            pltpu.VMEM(blocks, bf16),
            dma((2,)), dma((2, all_heads)), dma((2, kv_heads)),
            dma((hid_sends,)), dma((2, 4, 2, n_seq)),
            dma((all_heads, n_seq)), dma((all_heads, n_seq)),
            dma((all_heads, n_seq)), dma((all_heads, n_seq)),
            dma((spare, 2, 4)), dma((near, 2, 4)), dma((near, 2)), dma((n_dp // 2, 2)),
            dma((kv_heads, 4)), dma((kv_heads, 4)),
            dma((kv_heads, 4)), dma((kv_heads, 4)),
            dma((kv_heads, 2)), dma((kv_heads, 2)),
            dma((kv_heads, n_seq)), dma((kv_heads, n_seq)),
            dma((kv_heads, n_seq)), dma((kv_heads, n_seq)),
            dma((kv_heads, near, 2, parts)), dma((kv_heads, near, 2, parts)),
            dma((kv_heads, spare, 2, parts)), dma((kv_heads, near, 2, parts)),
        ],
        compiler_params=pltpu.CompilerParams(
            collective_id=0, has_side_effects=True, vmem_limit_bytes=VMEM_LIMIT
        ),
        name="attention_step",
    )(hidden[0], queries[0], key_matrix, value_matrix, out_grad[0],
      cos, sin, cos.T.copy(), sin.T.copy())
    attn_out, query_grad, key_grad, val_grad = put_all(
        attn_out, query_grad, key_grad, val_grad
    )
    return attn_out[None], query_grad[None], key_grad, val_grad


def solution(mesh):
    n_dp, n_seq = mesh.shape["dp"], mesh.shape["seq"]
    tokens, weights = P("dp", None, "seq", None), P("dp", "seq")
    return jax.shard_map(
        functools.partial(local, n_seq, n_dp),
        mesh=mesh,
        in_specs=(tokens, tokens, weights, weights, tokens),
        out_specs=(tokens, tokens, weights, weights),
        check_vma=False,
    )
```

```python
import functools
import math

import jax
import jax.numpy as jnp
import numpy as np
from jax import lax
from jax.experimental import pallas as pl
from jax.experimental.pallas import tpu as pltpu
from jax.sharding import PartitionSpec as P

HEAD_WIDTH = 128
ROPE_BASE = 500000.0
CORES = 2
MESH = pl.DeviceIdType.MESH
ANY = pl.BlockSpec(memory_space=pl.ANY)
VMEM = pl.BlockSpec(memory_space=pltpu.VMEM)
VMEM_LIMIT = 56 << 20
TILE = 1024


def grid_of(count):
    rows = 2 if count % 2 == 0 else 1
    return rows, count // rows


def place(n_seq, n_dp):
    dp, seq = lax.axis_index("dp"), lax.axis_index("seq")
    chips = n_dp // CORES
    chip, core = lax.div(dp, CORES), lax.rem(dp, CORES)
    rows, cols = grid_of(n_seq)
    row, col = lax.div(seq, cols), lax.rem(seq, cols)
    row_peers = [row * cols + lax.rem(col + d, cols) for d in range(1, cols)]
    col_peers = [lax.rem(row + d, rows) * cols + col for d in range(1, rows)]
    far_peers = [
        lax.rem(row + e, rows) * cols + lax.rem(col + d, cols)
        for e in range(1, rows)
        for d in range(1, cols)
    ]
    return dp, seq, chips, chip, core, row_peers, col_peers, far_peers


def kernel(
    n_seq, n_dp, kv_heads, group, tile,
    hidden, queries, key_matrix, value_matrix, out_grad, cos_in, sin_in, cos_t_in, sin_t_in,
    attn_out, qgrad_out, key_grad, val_grad,
    hid, qry, grd, key_all, val_all, sum_k, sum_v, raw_k, raw_v, raw_h, in_k, in_v,
    keys, vals, attn, qgrad, pre_t, pre_in,
    key_acc, val_acc, acc, mate_acc, mate_out, mate_in, far_out, far_in,
    cos, sin, cos_t, sin_t,
    load_sem, own_sem, store_sem, hid_send, hid_recv, qry_send, qry_recv, grd_send, grd_recv,
    far_w_send, far_w_recv, mate_w_send, w_recv, k_send, k_recv, v_send, v_recv, pre_send, pre_recv,
    a_send, a_recv, q_send, q_recv, mate_send, mate_recv, far_send, far_recv,
):
    f32, bf16 = jnp.float32, jnp.bfloat16
    dp, seq, chips, chip, core, row_peers, col_peers, far_peers = place(n_seq, n_dp)
    peers = row_peers + col_peers + far_peers
    near = chips // 2
    side, slot_w = lax.div(chip, near), lax.rem(chip, near)
    mate = chip * CORES + 1 - core
    twin = ((1 - side) * near + slot_w) * CORES + core
    others = [lax.rem(slot_w + d, near) for d in range(1, near)]

    def owner(w):
        return (side * near + w) * CORES + core

    wide = group * HEAD_WIDTH
    width = kv_heads * wide
    total = keys.shape[0]
    half = HEAD_WIDTH // 2
    block = total // 2
    deep = key_all.shape[1]
    quarter = hid.shape[-1]
    per = quarter // deep
    mine = slot_w * CORES + core
    tokens = hid.shape[4]
    piece_len = tokens // 2
    turns = ((0, 0), (0, 1), (1, 0), (0, 2), (1, 1), (1, 2), (1, 3), (0, 3))

    def stretch_of(c):
        return c // 2, pl.ds(c % 2 * piece_len, piece_len)

    barrier = pltpu.get_barrier_semaphore()
    greeted = [(dp, p) for p in peers] + [(mate, seq), (twin, seq)]
    greeted += [(owner(w), seq) for w in others]
    for device in greeted:
        pl.semaphore_signal(barrier, inc=1, device_id=device, device_id_type=MESH)
    pl.semaphore_wait(barrier, len(greeted))

    def head_cols(target, kv):
        return pl.ds(pl.multiple_of(target * width + kv * wide, wide), wide)

    def one_head(target, h):
        start = pl.multiple_of(target * width + h * HEAD_WIDTH, HEAD_WIDTH)
        return pl.ds(start, HEAD_WIDTH)

    def embed_cols(which, j):
        return pl.ds(pl.multiple_of((which * 2 + j) * quarter, quarter), quarter)

    loads = [
        (key_matrix, key_all.at[mine], load_sem.at[0]),
        (value_matrix, val_all.at[mine], load_sem.at[1]),
        (cos_in, cos, load_sem.at[2]),
        (sin_in, sin, load_sem.at[3]),
        (cos_t_in, cos_t, load_sem.at[4]),
        (sin_t_in, sin_t, load_sem.at[5]),
    ]
    for c in range(4):
        e, at = stretch_of(c)
        for j in range(2):
            pltpu.make_async_copy(
                hidden.at[e, at, embed_cols(side, j)], hid.at[0, j, e, seq, at],
                hid_recv.at[0, c, j, seq],
            ).start()

    def own_loads(h):
        return (
            (queries.at[:, :, one_head(seq, h)], qry.at[h, :, seq], own_sem.at[0, h]),
            (out_grad.at[:, :, one_head(seq, h)], grd.at[h, :, seq], own_sem.at[1, h]),
        )

    sends = []

    def start(copy):
        copy.start()
        sends.append(copy)

    slots = iter(range(hid_send.shape[0]))

    def hidden_copy(slot, c, j, source, target_dp, target, send_sem, src=None):
        e, at = stretch_of(c)
        dst = hid.at[slot, j, e, source, at]
        return pltpu.make_async_remote_copy(
            src_ref=dst if src is None else src, dst_ref=dst,
            send_sem=send_sem, recv_sem=hid_recv.at[slot, c, j, source],
            device_id=(target_dp, target), device_id_type=MESH,
        )

    def send_hidden(slot, c, j, source, target, src=None):
        start(hidden_copy(slot, c, j, source, dp, target, hid_send.at[next(slots)], src))

    def wait_hidden(slot, c, j, source):
        hidden_copy(slot, c, j, source, dp, source, hid_send.at[0]).wait_recv()

    def direct(p):
        slot, c = turns[p]
        e, at = stretch_of(c)
        if slot == 1:
            for j in range(2):
                wait_hidden(slot, c, j, seq)

        def source(j):
            return None if slot == 1 else hidden.at[e, at, embed_cols(side, j)]

        for j in range(2):
            for q in row_peers:
                send_hidden(slot, c, j, seq, q, source(j))
            for q in col_peers:
                send_hidden(slot, c, 1 - j, seq, q, source(1 - j))

    def relay_hidden(p):
        slot, c = turns[p]
        for r in row_peers:
            wait_hidden(slot, c, 0, r)
            for q in col_peers:
                send_hidden(slot, c, 0, r, q)
        for r in col_peers:
            wait_hidden(slot, c, 1, r)
            for q in row_peers:
                send_hidden(slot, c, 1, r, q)

    def wait_rest(p):
        slot, c = turns[p]
        for r in row_peers:
            wait_hidden(slot, c, 1, r)
        for r in col_peers:
            wait_hidden(slot, c, 0, r)
        for r in far_peers:
            wait_hidden(slot, c, 0, r)
            wait_hidden(slot, c, 1, r)

    tables = (key_all, val_all)
    owns = (key_matrix, value_matrix)

    def weight_copy(kind, piece, target_dp, send_sem, own=False):
        return pltpu.make_async_remote_copy(
            src_ref=owns[kind] if own else tables[kind].at[piece],
            dst_ref=tables[kind].at[piece],
            send_sem=send_sem, recv_sem=w_recv.at[piece, kind],
            device_id=(target_dp, seq), device_id_type=MESH,
        )

    strip = deep // 4

    def far_weight(kind, r, i, w, source):
        at = pl.ds(r * strip, strip)
        return pltpu.make_async_remote_copy(
            src_ref=owns[kind].at[at], dst_ref=tables[kind].at[source * CORES + core, at],
            send_sem=far_w_send.at[i, kind, r], recv_sem=far_w_recv.at[source, kind, r],
            device_id=(owner(w), seq), device_id_type=MESH,
        )

    def relay_weights(kind):
        for i, w in enumerate(others):
            for r in range(4):
                far_weight(kind, r, i, w, w).wait_recv()
            start(weight_copy(kind, w * CORES + core, mate, mate_w_send.at[i + 1, kind]))

    def wait_weights():
        for w in [slot_w] + others:
            for kind in range(2):
                piece = w * CORES + 1 - core
                weight_copy(kind, piece, mate, mate_w_send.at[0, kind]).wait_recv()

    def exchange(h, src, dst, send_sem, recv_sem):
        for i, p in enumerate(peers):
            start(pltpu.make_async_remote_copy(
                src_ref=src.at[:, :, one_head(p, h)], dst_ref=dst.at[h, :, seq],
                send_sem=send_sem.at[h, i], recv_sem=recv_sem.at[h, seq],
                device_id=(dp, p), device_id_type=MESH,
            ))

    def wait_exchange(h, dst, send_sem, recv_sem):
        for p in peers:
            pltpu.make_async_remote_copy(
                src_ref=dst.at[h, :, p], dst_ref=dst.at[h, :, p],
                send_sem=send_sem.at[h, 0], recv_sem=recv_sem.at[h, p],
                device_id=(dp, p), device_id_type=MESH,
            ).wait_recv()

    def project(p):
        slot, c = turns[p]
        e, at_rows = stretch_of(c)
        wait_rest(p)
        if slot == 0:
            for j in range(2):
                wait_hidden(slot, c, j, seq)
        sum_k[...] = jnp.zeros_like(sum_k)
        sum_v[...] = jnp.zeros_like(sum_v)

        @pl.loop(0, 2 * per)
        def _(i):
            j, at = lax.div(i, per), lax.rem(i, per)
            cols = pl.ds(pl.multiple_of(at * deep, deep), deep)
            rows = hid[slot, j, e, :, at_rows, cols].reshape(n_seq * piece_len, deep)
            sum_k[...] += jnp.dot(rows, key_all[i], preferred_element_type=f32)
            sum_v[...] += jnp.dot(rows, val_all[i], preferred_element_type=f32)

        shape = (n_seq, piece_len, HEAD_WIDTH)
        for kv in range(kv_heads):
            lanes = pl.ds(kv * HEAD_WIDTH, HEAD_WIDTH)
            raw_k[slot, kv, e, :, at_rows, :] = sum_k[:, lanes].reshape(shape)
            raw_v[slot, kv, e, :, at_rows, :] = sum_v[:, lanes].reshape(shape)
            raw_h[slot, kv, e, :, at_rows, :] = sum_v[:, lanes].reshape(shape).astype(bf16)
        if slot == 1:
            for kv in range(kv_heads):
                for copy in raw_copies(kv, c):
                    start(copy)

    def raw_copies(kv, c):
        e, at = stretch_of(c)
        return [
            pltpu.make_async_remote_copy(
                src_ref=src.at[1, kv, e, :, at], dst_ref=dst.at[kv, e, :, at],
                send_sem=send_sem.at[kv, c], recv_sem=recv_sem.at[kv, c],
                device_id=(twin, seq), device_id_type=MESH,
            )
            for src, dst, send_sem, recv_sem in (
                (raw_k, in_k, k_send, k_recv), (raw_h, in_v, v_send, v_recv),
            )
        ]

    def settle(kv):
        lanes = pl.ds(kv * HEAD_WIDTH, HEAD_WIDTH)
        for c in range(4):
            for copy in raw_copies(kv, c):
                copy.wait_recv()
        flat = (total, HEAD_WIDTH)
        raw = raw_k[0, kv].reshape(flat) + in_k[kv].reshape(flat)
        swapped = jnp.concatenate([raw[:, half:], raw[:, :half]], axis=1)
        keys[:, lanes] = (raw * cos[...] + swapped * sin[...]).astype(bf16)
        vals[:, lanes] = (raw_v[0, kv].reshape(flat) + in_v[kv].reshape(flat).astype(f32)).astype(bf16)

    scale = 1.0 / math.sqrt(HEAD_WIDTH)
    nt = (((1,), (1,)), ((), ()))
    tn = (((0,), (0,)), ((), ()))

    pack = 2 if group % 2 == 0 else 1
    half_seq = n_seq // 2
    rows_n = half_seq * tokens
    tri_shape = (pack * rows_n, rows_n)
    tri_row = lax.rem(lax.broadcasted_iota(jnp.int32, tri_shape, 0), rows_n)
    tri = lax.broadcasted_iota(jnp.int32, tri_shape, 1) <= tri_row

    def attend(kv, between=None):
        lanes = pl.ds(kv * HEAD_WIDTH, HEAD_WIDTH)
        key_acc[...] = jnp.zeros_like(key_acc)
        val_acc[...] = jnp.zeros_like(val_acc)

        @pl.loop(0, group // pack)
        def _(m):
            first = kv * group + m * pack
            if between is not None:
                pl.when(m == group // pack - 1)(between)
            for n in range(pack):
                h = first + n
                wait_exchange(h, qry, qry_send, qry_recv)
                wait_exchange(h, grd, grd_send, grd_recv)
                for copy in own_loads(h):
                    pltpu.make_async_copy(*copy).wait()
            for b in range(4):
                span, seqs = (b + 1) * rows_n, pl.ds(b % 2 * half_seq, half_seq)
                flat = (pack * rows_n, HEAD_WIDTH)
                q = qry[pl.ds(first, pack), b // 2, seqs].reshape(flat)
                g = grd[pl.ds(first, pack), b // 2, seqs].reshape(flat)
                k, v = keys[:span, lanes], vals[:span, lanes]
                s = lax.dot_general(q, k, nt, preferred_element_type=f32) * scale
                last = jnp.where(tri, s[:, span - rows_n:], -jnp.inf)
                s = last if b == 0 else jnp.concatenate([s[:, :span - rows_n], last], axis=1)
                e = jnp.exp(s - jnp.max(s, axis=1, keepdims=True))
                p = e * (1.0 / jnp.sum(e, axis=1, keepdims=True))
                p_half = p.astype(bf16)
                o = jnp.dot(p_half, v, preferred_element_type=f32).astype(bf16)
                dot = jnp.sum(g.astype(f32) * o.astype(f32), axis=1, keepdims=True)
                gp = lax.dot_general(g, v, nt, preferred_element_type=f32)
                ds = (p * (gp - dot) * scale).astype(bf16)
                dq = jnp.dot(ds, k, preferred_element_type=f32).astype(bf16)
                for n in range(pack):
                    start_n = pl.multiple_of((m * pack + n) * HEAD_WIDTH, HEAD_WIDTH)
                    head = pl.ds(start_n, HEAD_WIDTH)
                    shape = (half_seq, tokens, HEAD_WIDTH)
                    rows = slice(n * rows_n, (n + 1) * rows_n)
                    attn[kv, b // 2, seqs, :, head] = o[rows].reshape(shape)
                    qgrad[kv, b // 2, seqs, :, head] = dq[rows].reshape(shape)
                key_acc[:, :span] += lax.dot_general(q, ds, tn, preferred_element_type=f32)
                val_acc[:, :span] += lax.dot_general(g, p_half, tn, preferred_element_type=f32)

        grown = key_acc[...]
        swapped = jnp.concatenate([grown[half:, :], grown[:half, :]], axis=0)
        pre_t[kv, 0] = (grown * cos_t[...] - swapped * sin_t[...]).astype(bf16)
        pre_t[kv, 1] = val_acc[...].astype(bf16)

    def pre_copy(kv, u):
        return pltpu.make_async_remote_copy(
            src_ref=pre_t.at[kv, u], dst_ref=pre_in.at[kv, u],
            send_sem=pre_send.at[kv, u], recv_sem=pre_recv.at[kv, u],
            device_id=(twin, seq), device_id_type=MESH,
        )

    depth = deep
    results = ((attn, attn_out, a_send, a_recv), (qgrad, qgrad_out, q_send, q_recv))

    def own_store(kv, which):
        src, dst, _, _ = results[which]
        return pltpu.make_async_copy(
            src.at[kv, :, seq], dst.at[:, :, head_cols(seq, kv)], store_sem.at[which, kv]
        )

    def give_back(kv):
        for which, (src, dst, send_sem, recv_sem) in enumerate(results):
            for i, p in enumerate(peers):
                start(pltpu.make_async_remote_copy(
                    src_ref=src.at[kv, :, p], dst_ref=dst.at[:, :, head_cols(seq, kv)],
                    send_sem=send_sem.at[kv, i], recv_sem=recv_sem.at[kv, seq],
                    device_id=(dp, p), device_id_type=MESH,
                ))
            own_store(kv, which).start()

    def wait_back(kv):
        for which, (src, dst, send_sem, recv_sem) in enumerate(results):
            for p in peers:
                pltpu.make_async_remote_copy(
                    src_ref=src.at[kv, :, p], dst_ref=dst.at[:, :, head_cols(p, kv)],
                    send_sem=send_sem.at[kv, 0], recv_sem=recv_sem.at[kv, p],
                    device_id=(dp, p), device_id_type=MESH,
                ).wait_recv()
            own_store(kv, which).wait()

    parts = depth // tile

    def mate_copy(kv, w, u, t):
        return pltpu.make_async_remote_copy(
            src_ref=mate_out.at[kv, w, u, t], dst_ref=mate_in.at[kv, w, u, t],
            send_sem=mate_send.at[kv, w, u, t], recv_sem=mate_recv.at[kv, w, u, t],
            device_id=(mate, seq), device_id_type=MESH,
        )

    def far_copy(kv, i, w, u, t, back=False):
        at = w if back else slot_w
        return pltpu.make_async_remote_copy(
            src_ref=far_out.at[kv, i, u, t], dst_ref=far_in.at[kv, at, u, t],
            send_sem=far_send.at[kv, i, u, t], recv_sem=far_recv.at[kv, at, u, t],
            device_id=(owner(w), seq), device_id_type=MESH,
        )

    def part_of(left, slot, piece, t):
        j, at = lax.div(piece, per), lax.rem(piece, per)
        cols = pl.ds(pl.multiple_of(at * depth + t * tile, tile), tile)
        rows = hid[slot, j, :, :, :, cols].reshape(total, tile)
        return jnp.dot(left, rows, preferred_element_type=f32)

    def own_products(kv):
        left = pre_t.at[kv]

        def both(piece, t):
            return part_of(left[...].reshape(2 * HEAD_WIDTH, total), 0, piece, t)

        for w in others + [slot_w]:
            @pl.loop(0, parts)
            def _(t):
                out = both(w * CORES + 1 - core, t)
                mate_acc[kv, w, 0, t] = out[:HEAD_WIDTH]
                mate_acc[kv, w, 1, t] = out[HEAD_WIDTH:]
                out = both(w * CORES + core, t)
                acc[kv, w, 0, t] = out[:HEAD_WIDTH]
                acc[kv, w, 1, t] = out[HEAD_WIDTH:]

    def twin_products(kv, u):
        def to_mate(w):
            @pl.loop(0, parts)
            def _(t):
                v = mate_acc[kv, w, u, t] + part_of(pre_in[kv, u], 1, w * CORES + 1 - core, t)
                mate_out[kv, w, u, t] = v.astype(bf16)
                mate_copy(kv, w, u, t).start()

        def to_acc(w):
            @pl.loop(0, parts)
            def _(t):
                acc[kv, w, u, t] += part_of(pre_in[kv, u], 1, w * CORES + core, t)

        pre_copy(kv, u).wait_recv()
        for w in others:
            to_mate(w)
        for w in others:
            to_acc(w)
        for i, w in enumerate(others):
            @pl.loop(0, parts)
            def _(t):
                mate_copy(kv, w, u, t).wait_recv()
                v = acc[kv, w, u, t] + mate_in[kv, w, u, t].astype(f32)
                far_out[kv, i, u, t] = v.astype(bf16)
                far_copy(kv, i, w, u, t).start()
        to_mate(slot_w)
        to_acc(slot_w)

    def finish(kv, u):
        lanes = pl.ds(kv * HEAD_WIDTH, HEAD_WIDTH)
        grad = val_grad if u else key_grad
        for t in range(parts):
            mate_copy(kv, slot_w, u, t).wait_recv()
            v = acc[kv, slot_w, u, t] + mate_in[kv, slot_w, u, t].astype(f32)
            for i, w in enumerate(others):
                far_copy(kv, i, w, u, t, True).wait_recv()
                v = v + far_in[kv, w, u, t].astype(f32)
            grad[pl.ds(t * tile, tile), lanes] = v.T

    for c in range(4):
        e, at = stretch_of(c)
        for j in range(2):
            src = hidden.at[e, at, embed_cols(1 - side, j)]
            start(hidden_copy(1, c, j, seq, twin, seq, hid_send.at[next(slots)], src))
            for i, w in enumerate(others):
                start(far_weight(c // 2, c % 2 * 2 + j, i, w, slot_w))
    for kind in range(2):
        start(weight_copy(kind, mine, mate, mate_w_send.at[0, kind], True))
    for copy in loads:
        pltpu.make_async_copy(*copy).start()
    direct(0)
    for h in range(kv_heads * group):
        for copy in own_loads(h):
            pltpu.make_async_copy(*copy).start()
    for p in range(5):
        direct(p + 1)
        relay_hidden(p)
        if p == 4:
            relay_weights(0)
    direct(6)
    relay_hidden(5)
    direct(7)
    relay_weights(1)
    for copy in loads:
        pltpu.make_async_copy(*copy).wait()
    wait_weights()
    project(2)
    project(4)
    relay_hidden(6)
    project(5)
    relay_hidden(7)
    for h in range(kv_heads * group):
        exchange(h, queries, qry, qry_send, qry_recv)
        exchange(h, out_grad, grd, grd_send, grd_recv)
    for p in (6, 0, 1, 3, 7):
        project(p)
    for kv in range(kv_heads):
        settle(kv)
        attend(kv, functools.partial(twin_products, kv - 1, 1) if kv else None)
        start(pre_copy(kv, 1))
        if kv:
            twin_products(kv - 1, 0)
        start(pre_copy(kv, 0))
        own_products(kv)
        give_back(kv)
    for u in (1, 0):
        twin_products(kv_heads - 1, u)
    for kv in range(kv_heads):
        for u in (1, 0):
            finish(kv, u)
        wait_back(kv)
    for kv in range(kv_heads):
        for u in range(2):
            for t in range(parts):
                for w in range(near):
                    mate_copy(kv, w, u, t).wait_send()
                for i, w in enumerate(others):
                    far_copy(kv, i, w, u, t).wait_send()
    for copy in sends:
        copy.wait_send()


def put_kernel(*refs):
    count = len(refs) // 2
    sem = refs[-1]
    copies = [
        pltpu.make_async_copy(refs[i], refs[count + i], sem.at[i]) for i in range(count)
    ]
    for copy in copies:
        copy.start()
    for copy in copies:
        copy.wait()


def put_all(*arrays):
    return pl.pallas_call(
        put_kernel,
        out_shape=[jax.ShapeDtypeStruct(x.shape, x.dtype) for x in arrays],
        in_specs=[pl.BlockSpec(memory_space=pltpu.VMEM)] * len(arrays),
        out_specs=[ANY] * len(arrays),
        scratch_shapes=[pltpu.SemaphoreType.DMA((len(arrays),))],
        compiler_params=pltpu.CompilerParams(vmem_limit_bytes=1 << 20),
        name="put_all",
    )(*arrays)


def local(n_seq, n_dp, hidden, queries, key_matrix, value_matrix, out_grad):
    _, stretches, tokens, embed = hidden.shape
    full = queries.shape[3]
    width = full // n_seq
    deep, kv_width = key_matrix.shape
    kv_heads = kv_width // HEAD_WIDTH
    group = width // kv_width
    wide = group * HEAD_WIDTH
    near = n_dp // CORES // 2
    quarter = embed // 4
    rows, cols = grid_of(n_seq)
    hid_sends = 8 * (2 * (rows - 1 + cols - 1) + 2 * (rows - 1) * (cols - 1)) + 8
    total = stretches * n_seq * tokens
    block = n_seq * tokens
    bf16, f32 = jnp.bfloat16, jnp.float32
    dma = pltpu.SemaphoreType.DMA
    half = HEAD_WIDTH // 2
    inverse = np.exp(
        np.arange(half, dtype=np.float32) * np.float32(-2.0 * math.log(ROPE_BASE) / HEAD_WIDTH)
    ).astype(np.float32)
    phase = np.arange(total, dtype=np.float32)[:, None] * inverse[None, :]
    cos_half, sin_half = np.cos(phase), np.sin(phase)
    cos = np.concatenate([cos_half, cos_half], axis=1).astype(np.float32)
    sin = np.concatenate([-sin_half, sin_half], axis=1).astype(np.float32)
    heads = (kv_heads, stretches, n_seq, tokens, wide)
    single = (kv_heads * group, stretches, n_seq, tokens, HEAD_WIDTH)
    tile = math.gcd(deep, TILE)
    parts = deep // tile
    blocks = (kv_heads, near, 2, parts, HEAD_WIDTH, tile)
    weights = (n_dp // 2, deep, kv_width)
    raw = (kv_heads, stretches, n_seq, tokens, HEAD_WIDTH)
    all_heads = kv_heads * group
    spare = max(near - 1, 1)
    attn_out, query_grad, key_grad, val_grad = pl.pallas_call(
        functools.partial(kernel, n_seq, n_dp, kv_heads, group, tile),
        out_shape=[
            pltpu.VMEM((stretches, tokens, full), bf16),
            pltpu.VMEM((stretches, tokens, full), bf16),
            pltpu.VMEM((deep, kv_width), f32),
            pltpu.VMEM((deep, kv_width), f32),
        ],
        in_specs=[ANY] * 9,
        out_specs=[VMEM] * 4,
        scratch_shapes=[
            pltpu.VMEM((2, 2, stretches, n_seq, tokens, quarter), bf16),
            pltpu.VMEM(single, bf16),
            pltpu.VMEM(single, bf16),
            pltpu.VMEM(weights, bf16),
            pltpu.VMEM(weights, bf16),
            pltpu.VMEM((block // 2, kv_width), f32),
            pltpu.VMEM((block // 2, kv_width), f32),
            pltpu.VMEM((2,) + raw, f32),
            pltpu.VMEM((2,) + raw, f32),
            pltpu.VMEM((2,) + raw, bf16),
            pltpu.VMEM(raw, f32),
            pltpu.VMEM(raw, bf16),
            pltpu.VMEM((total, kv_width), bf16),
            pltpu.VMEM((total, kv_width), bf16),
            pltpu.VMEM(heads, bf16),
            pltpu.VMEM(heads, bf16),
            pltpu.VMEM((kv_heads, 2, HEAD_WIDTH, total), bf16),
            pltpu.VMEM((kv_heads, 2, HEAD_WIDTH, total), bf16),
            pltpu.VMEM((HEAD_WIDTH, total), f32),
            pltpu.VMEM((HEAD_WIDTH, total), f32),
            pltpu.VMEM(blocks, f32),
            pltpu.VMEM(blocks, f32),
            pltpu.VMEM(blocks, bf16),
            pltpu.VMEM(blocks, bf16),
            pltpu.VMEM((kv_heads, spare, 2, parts, HEAD_WIDTH, tile), bf16),
            pltpu.VMEM(blocks, bf16),
            pltpu.VMEM((total, HEAD_WIDTH), f32),
            pltpu.VMEM((total, HEAD_WIDTH), f32),
            pltpu.VMEM((HEAD_WIDTH, total), f32),
            pltpu.VMEM((HEAD_WIDTH, total), f32),
            dma((6,)), dma((2, all_heads)), dma((2, kv_heads)),
            dma((hid_sends,)), dma((2, 4, 2, n_seq)),
            dma((all_heads, n_seq)), dma((all_heads, n_seq)),
            dma((all_heads, n_seq)), dma((all_heads, n_seq)),
            dma((spare, 2, 4)), dma((near, 2, 4)), dma((near, 2)), dma((n_dp // 2, 2)),
            dma((kv_heads, 4)), dma((kv_heads, 4)),
            dma((kv_heads, 4)), dma((kv_heads, 4)),
            dma((kv_heads, 2)), dma((kv_heads, 2)),
            dma((kv_heads, n_seq)), dma((kv_heads, n_seq)),
            dma((kv_heads, n_seq)), dma((kv_heads, n_seq)),
            dma((kv_heads, near, 2, parts)), dma((kv_heads, near, 2, parts)),
            dma((kv_heads, spare, 2, parts)), dma((kv_heads, near, 2, parts)),
        ],
        compiler_params=pltpu.CompilerParams(
            collective_id=0, has_side_effects=True, vmem_limit_bytes=VMEM_LIMIT
        ),
        name="attention_step",
    )(hidden[0], queries[0], key_matrix, value_matrix, out_grad[0],
      cos, sin, cos.T.copy(), sin.T.copy())
    attn_out, query_grad, key_grad, val_grad = put_all(
        attn_out, query_grad, key_grad, val_grad
    )
    return attn_out[None], query_grad[None], key_grad, val_grad


def solution(mesh):
    n_dp, n_seq = mesh.shape["dp"], mesh.shape["seq"]
    tokens, weights = P("dp", None, "seq", None), P("dp", "seq")
    return jax.shard_map(
        functools.partial(local, n_seq, n_dp),
        mesh=mesh,
        in_specs=(tokens, tokens, weights, weights, tokens),
        out_specs=(tokens, tokens, weights, weights),
        check_vma=False,
    )
```

```python
import functools
import math

import jax
import jax.numpy as jnp
import numpy as np
from jax import lax
from jax.experimental import pallas as pl
from jax.experimental.pallas import tpu as pltpu
from jax.sharding import PartitionSpec as P

HEAD_WIDTH = 128
ROPE_BASE = 500000.0
CORES = 2
MESH = pl.DeviceIdType.MESH
ANY = pl.BlockSpec(memory_space=pl.ANY)
VMEM = pl.BlockSpec(memory_space=pltpu.VMEM)
VMEM_LIMIT = 56 << 20
TILE = 1024


def grid_of(count):
    rows = 2 if count % 2 == 0 else 1
    return rows, count // rows


def place(n_seq, n_dp):
    dp, seq = lax.axis_index("dp"), lax.axis_index("seq")
    chips = n_dp // CORES
    chip, core = lax.div(dp, CORES), lax.rem(dp, CORES)
    rows, cols = grid_of(n_seq)
    row, col = lax.div(seq, cols), lax.rem(seq, cols)
    row_peers = [row * cols + lax.rem(col + d, cols) for d in range(1, cols)]
    col_peers = [lax.rem(row + d, rows) * cols + col for d in range(1, rows)]
    far_peers = [
        lax.rem(row + e, rows) * cols + lax.rem(col + d, cols)
        for e in range(1, rows)
        for d in range(1, cols)
    ]
    return dp, seq, chips, chip, core, row_peers, col_peers, far_peers


def kernel(
    n_seq, n_dp, kv_heads, group, tile,
    hidden, queries, key_matrix, value_matrix, out_grad, cos_in, sin_in, cos_t_in, sin_t_in,
    attn_out, qgrad_out, key_grad, val_grad,
    hid, qry, grd, key_all, val_all, sum_k, sum_v, raw_k, raw_v, raw_h, in_k, in_v,
    keys, vals, attn, qgrad, pre_t, pre_in,
    key_acc, val_acc, acc, mate_acc, mate_out, mate_in, far_out, far_in,
    cos, sin, cos_t, sin_t,
    load_sem, own_sem, store_sem, hid_send, hid_recv, qry_send, qry_recv, grd_send, grd_recv,
    far_w_send, far_w_recv, mate_w_send, w_recv, k_send, k_recv, v_send, v_recv, pre_send, pre_recv,
    a_send, a_recv, q_send, q_recv, mate_send, mate_recv, far_send, far_recv,
):
    f32, bf16 = jnp.float32, jnp.bfloat16
    dp, seq, chips, chip, core, row_peers, col_peers, far_peers = place(n_seq, n_dp)
    peers = row_peers + col_peers + far_peers
    near = chips // 2
    side, slot_w = lax.div(chip, near), lax.rem(chip, near)
    mate = chip * CORES + 1 - core
    twin = ((1 - side) * near + slot_w) * CORES + core
    others = [lax.rem(slot_w + d, near) for d in range(1, near)]

    def owner(w):
        return (side * near + w) * CORES + core

    wide = group * HEAD_WIDTH
    width = kv_heads * wide
    total = keys.shape[0]
    half = HEAD_WIDTH // 2
    block = total // 2
    deep = key_all.shape[1]
    quarter = hid.shape[-1]
    per = quarter // deep
    mine = slot_w * CORES + core
    tokens = hid.shape[4]
    piece_len = tokens // 2
    turns = ((0, 0), (0, 1), (1, 0), (0, 2), (1, 1), (1, 2), (1, 3), (0, 3))

    def stretch_of(c):
        return c // 2, pl.ds(c % 2 * piece_len, piece_len)

    barrier = pltpu.get_barrier_semaphore()
    greeted = [(dp, p) for p in peers] + [(mate, seq), (twin, seq)]
    greeted += [(owner(w), seq) for w in others]
    for device in greeted:
        pl.semaphore_signal(barrier, inc=1, device_id=device, device_id_type=MESH)

    def head_cols(target, kv):
        return pl.ds(pl.multiple_of(target * width + kv * wide, wide), wide)

    def one_head(target, h):
        start = pl.multiple_of(target * width + h * HEAD_WIDTH, HEAD_WIDTH)
        return pl.ds(start, HEAD_WIDTH)

    def embed_cols(which, j):
        return pl.ds(pl.multiple_of((which * 2 + j) * quarter, quarter), quarter)

    loads = [
        (key_matrix, key_all.at[mine], load_sem.at[0]),
        (value_matrix, val_all.at[mine], load_sem.at[1]),
        (cos_in, cos, load_sem.at[2]),
        (sin_in, sin, load_sem.at[3]),
        (cos_t_in, cos_t, load_sem.at[4]),
        (sin_t_in, sin_t, load_sem.at[5]),
    ]
    for c in range(4):
        e, at = stretch_of(c)
        for j in range(2):
            pltpu.make_async_copy(
                hidden.at[e, at, embed_cols(side, j)], hid.at[0, j, e, seq, at],
                hid_recv.at[0, c, j, seq],
            ).start()

    for copy in loads:
        pltpu.make_async_copy(*copy).start()
    pl.semaphore_wait(barrier, len(greeted))

    def own_loads(h):
        return (
            (queries.at[:, :, one_head(seq, h)], qry.at[h, :, seq], own_sem.at[0, h]),
            (out_grad.at[:, :, one_head(seq, h)], grd.at[h, :, seq], own_sem.at[1, h]),
        )

    sends = []

    def start(copy):
        copy.start()
        sends.append(copy)

    slots = iter(range(hid_send.shape[0]))

    def hidden_copy(slot, c, j, source, target_dp, target, send_sem, src=None):
        e, at = stretch_of(c)
        dst = hid.at[slot, j, e, source, at]
        return pltpu.make_async_remote_copy(
            src_ref=dst if src is None else src, dst_ref=dst,
            send_sem=send_sem, recv_sem=hid_recv.at[slot, c, j, source],
            device_id=(target_dp, target), device_id_type=MESH,
        )

    def send_hidden(slot, c, j, source, target, src=None):
        start(hidden_copy(slot, c, j, source, dp, target, hid_send.at[next(slots)], src))

    def wait_hidden(slot, c, j, source):
        hidden_copy(slot, c, j, source, dp, source, hid_send.at[0]).wait_recv()

    def direct(p):
        slot, c = turns[p]
        e, at = stretch_of(c)
        if slot == 1:
            for j in range(2):
                wait_hidden(slot, c, j, seq)

        def source(j):
            return None if slot == 1 else hidden.at[e, at, embed_cols(side, j)]

        for j in range(2):
            for q in row_peers:
                send_hidden(slot, c, j, seq, q, source(j))
            for q in col_peers:
                send_hidden(slot, c, 1 - j, seq, q, source(1 - j))

    def relay_hidden(p):
        slot, c = turns[p]
        for r in row_peers:
            wait_hidden(slot, c, 0, r)
            for q in col_peers:
                send_hidden(slot, c, 0, r, q)
        for r in col_peers:
            wait_hidden(slot, c, 1, r)
            for q in row_peers:
                send_hidden(slot, c, 1, r, q)

    def wait_rest(p):
        slot, c = turns[p]
        for r in row_peers:
            wait_hidden(slot, c, 1, r)
        for r in col_peers:
            wait_hidden(slot, c, 0, r)
        for r in far_peers:
            wait_hidden(slot, c, 0, r)
            wait_hidden(slot, c, 1, r)

    tables = (key_all, val_all)
    owns = (key_matrix, value_matrix)

    def weight_copy(kind, piece, target_dp, send_sem, own=False):
        return pltpu.make_async_remote_copy(
            src_ref=owns[kind] if own else tables[kind].at[piece],
            dst_ref=tables[kind].at[piece],
            send_sem=send_sem, recv_sem=w_recv.at[piece, kind],
            device_id=(target_dp, seq), device_id_type=MESH,
        )

    strip = deep // 4

    def far_weight(kind, r, i, w, source):
        at = pl.ds(r * strip, strip)
        return pltpu.make_async_remote_copy(
            src_ref=owns[kind].at[at], dst_ref=tables[kind].at[source * CORES + core, at],
            send_sem=far_w_send.at[i, kind, r], recv_sem=far_w_recv.at[source, kind, r],
            device_id=(owner(w), seq), device_id_type=MESH,
        )

    def relay_weights(kind):
        for i, w in enumerate(others):
            for r in range(4):
                far_weight(kind, r, i, w, w).wait_recv()
            start(weight_copy(kind, w * CORES + core, mate, mate_w_send.at[i + 1, kind]))

    def wait_weights():
        for w in [slot_w] + others:
            for kind in range(2):
                piece = w * CORES + 1 - core
                weight_copy(kind, piece, mate, mate_w_send.at[0, kind]).wait_recv()

    def exchange(h, src, dst, send_sem, recv_sem):
        for i, p in enumerate(peers):
            start(pltpu.make_async_remote_copy(
                src_ref=src.at[:, :, one_head(p, h)], dst_ref=dst.at[h, :, seq],
                send_sem=send_sem.at[h, i], recv_sem=recv_sem.at[h, seq],
                device_id=(dp, p), device_id_type=MESH,
            ))

    def wait_exchange(h, dst, send_sem, recv_sem):
        for p in peers:
            pltpu.make_async_remote_copy(
                src_ref=dst.at[h, :, p], dst_ref=dst.at[h, :, p],
                send_sem=send_sem.at[h, 0], recv_sem=recv_sem.at[h, p],
                device_id=(dp, p), device_id_type=MESH,
            ).wait_recv()

    def project(p):
        slot, c = turns[p]
        e, at_rows = stretch_of(c)
        wait_rest(p)
        if slot == 0:
            for j in range(2):
                wait_hidden(slot, c, j, seq)
        sum_k[...] = jnp.zeros_like(sum_k)
        sum_v[...] = jnp.zeros_like(sum_v)

        @pl.loop(0, 2 * per)
        def _(i):
            j, at = lax.div(i, per), lax.rem(i, per)
            cols = pl.ds(pl.multiple_of(at * deep, deep), deep)
            rows = hid[slot, j, e, :, at_rows, cols].reshape(n_seq * piece_len, deep)
            sum_k[...] += jnp.dot(rows, key_all[i], preferred_element_type=f32)
            sum_v[...] += jnp.dot(rows, val_all[i], preferred_element_type=f32)

        shape = (n_seq, piece_len, HEAD_WIDTH)
        for kv in range(kv_heads):
            lanes = pl.ds(kv * HEAD_WIDTH, HEAD_WIDTH)
            raw_k[slot, kv, e, :, at_rows, :] = sum_k[:, lanes].reshape(shape)
            raw_v[slot, kv, e, :, at_rows, :] = sum_v[:, lanes].reshape(shape)
            raw_h[slot, kv, e, :, at_rows, :] = sum_v[:, lanes].reshape(shape).astype(bf16)
        if slot == 1:
            for kv in range(kv_heads):
                for copy in raw_copies(kv, c):
                    start(copy)

    def raw_copies(kv, c):
        e, at = stretch_of(c)
        return [
            pltpu.make_async_remote_copy(
                src_ref=src.at[1, kv, e, :, at], dst_ref=dst.at[kv, e, :, at],
                send_sem=send_sem.at[kv, c], recv_sem=recv_sem.at[kv, c],
                device_id=(twin, seq), device_id_type=MESH,
            )
            for src, dst, send_sem, recv_sem in (
                (raw_k, in_k, k_send, k_recv), (raw_h, in_v, v_send, v_recv),
            )
        ]

    def settle(kv):
        lanes = pl.ds(kv * HEAD_WIDTH, HEAD_WIDTH)
        for c in range(4):
            for copy in raw_copies(kv, c):
                copy.wait_recv()
        flat = (total, HEAD_WIDTH)
        raw = raw_k[0, kv].reshape(flat) + in_k[kv].reshape(flat)
        swapped = jnp.concatenate([raw[:, half:], raw[:, :half]], axis=1)
        keys[:, lanes] = (raw * cos[...] + swapped * sin[...]).astype(bf16)
        vals[:, lanes] = (raw_v[0, kv].reshape(flat) + in_v[kv].reshape(flat).astype(f32)).astype(bf16)

    scale = 1.0 / math.sqrt(HEAD_WIDTH)
    nt = (((1,), (1,)), ((), ()))
    tn = (((0,), (0,)), ((), ()))

    pack = 2 if group % 2 == 0 else 1
    half_seq = n_seq // 2
    rows_n = half_seq * tokens
    tri_shape = (pack * rows_n, rows_n)
    tri_row = lax.rem(lax.broadcasted_iota(jnp.int32, tri_shape, 0), rows_n)
    tri = lax.broadcasted_iota(jnp.int32, tri_shape, 1) <= tri_row

    def attend(kv, between=None):
        lanes = pl.ds(kv * HEAD_WIDTH, HEAD_WIDTH)
        key_acc[...] = jnp.zeros_like(key_acc)
        val_acc[...] = jnp.zeros_like(val_acc)

        @pl.loop(0, group // pack)
        def _(m):
            first = kv * group + m * pack
            if between is not None:
                pl.when(m == group // pack - 1)(between)
            for n in range(pack):
                h = first + n
                wait_exchange(h, qry, qry_send, qry_recv)
                wait_exchange(h, grd, grd_send, grd_recv)
                for copy in own_loads(h):
                    pltpu.make_async_copy(*copy).wait()
            for b in range(4):
                span, seqs = (b + 1) * rows_n, pl.ds(b % 2 * half_seq, half_seq)
                flat = (pack * rows_n, HEAD_WIDTH)
                q = qry[pl.ds(first, pack), b // 2, seqs].reshape(flat)
                g = grd[pl.ds(first, pack), b // 2, seqs].reshape(flat)
                k, v = keys[:span, lanes], vals[:span, lanes]
                s = lax.dot_general(q, k, nt, preferred_element_type=f32) * scale
                last = jnp.where(tri, s[:, span - rows_n:], -jnp.inf)
                s = last if b == 0 else jnp.concatenate([s[:, :span - rows_n], last], axis=1)
                e = jnp.exp(s - jnp.max(s, axis=1, keepdims=True))
                p = e * (1.0 / jnp.sum(e, axis=1, keepdims=True))
                p_half = p.astype(bf16)
                o = jnp.dot(p_half, v, preferred_element_type=f32).astype(bf16)
                dot = jnp.sum(g.astype(f32) * o.astype(f32), axis=1, keepdims=True)
                gp = lax.dot_general(g, v, nt, preferred_element_type=f32)
                ds = (p * (gp - dot) * scale).astype(bf16)
                dq = jnp.dot(ds, k, preferred_element_type=f32).astype(bf16)
                for n in range(pack):
                    start_n = pl.multiple_of((m * pack + n) * HEAD_WIDTH, HEAD_WIDTH)
                    head = pl.ds(start_n, HEAD_WIDTH)
                    shape = (half_seq, tokens, HEAD_WIDTH)
                    rows = slice(n * rows_n, (n + 1) * rows_n)
                    attn[kv, b // 2, seqs, :, head] = o[rows].reshape(shape)
                    qgrad[kv, b // 2, seqs, :, head] = dq[rows].reshape(shape)
                key_acc[:, :span] += lax.dot_general(q, ds, tn, preferred_element_type=f32)
                val_acc[:, :span] += lax.dot_general(g, p_half, tn, preferred_element_type=f32)

        grown = key_acc[...]
        swapped = jnp.concatenate([grown[half:, :], grown[:half, :]], axis=0)
        pre_t[kv, 0] = (grown * cos_t[...] - swapped * sin_t[...]).astype(bf16)
        pre_t[kv, 1] = val_acc[...].astype(bf16)

    def pre_copy(kv, u):
        return pltpu.make_async_remote_copy(
            src_ref=pre_t.at[kv, u], dst_ref=pre_in.at[kv, u],
            send_sem=pre_send.at[kv, u], recv_sem=pre_recv.at[kv, u],
            device_id=(twin, seq), device_id_type=MESH,
        )

    depth = deep
    results = ((attn, attn_out, a_send, a_recv), (qgrad, qgrad_out, q_send, q_recv))

    def own_store(kv, which):
        src, dst, _, _ = results[which]
        return pltpu.make_async_copy(
            src.at[kv, :, seq], dst.at[:, :, head_cols(seq, kv)], store_sem.at[which, kv]
        )

    def give_back(kv):
        for which, (src, dst, send_sem, recv_sem) in enumerate(results):
            for i, p in enumerate(peers):
                start(pltpu.make_async_remote_copy(
                    src_ref=src.at[kv, :, p], dst_ref=dst.at[:, :, head_cols(seq, kv)],
                    send_sem=send_sem.at[kv, i], recv_sem=recv_sem.at[kv, seq],
                    device_id=(dp, p), device_id_type=MESH,
                ))
            own_store(kv, which).start()

    def wait_back(kv):
        for which, (src, dst, send_sem, recv_sem) in enumerate(results):
            for p in peers:
                pltpu.make_async_remote_copy(
                    src_ref=src.at[kv, :, p], dst_ref=dst.at[:, :, head_cols(p, kv)],
                    send_sem=send_sem.at[kv, 0], recv_sem=recv_sem.at[kv, p],
                    device_id=(dp, p), device_id_type=MESH,
                ).wait_recv()
            own_store(kv, which).wait()

    parts = depth // tile

    def mate_copy(kv, w, u, t):
        return pltpu.make_async_remote_copy(
            src_ref=mate_out.at[kv, w, u, t], dst_ref=mate_in.at[kv, w, u, t],
            send_sem=mate_send.at[kv, w, u, t], recv_sem=mate_recv.at[kv, w, u, t],
            device_id=(mate, seq), device_id_type=MESH,
        )

    def far_copy(kv, i, w, u, t, back=False):
        at = w if back else slot_w
        return pltpu.make_async_remote_copy(
            src_ref=far_out.at[kv, i, u, t], dst_ref=far_in.at[kv, at, u, t],
            send_sem=far_send.at[kv, i, u, t], recv_sem=far_recv.at[kv, at, u, t],
            device_id=(owner(w), seq), device_id_type=MESH,
        )

    def part_of(left, slot, piece, t):
        j, at = lax.div(piece, per), lax.rem(piece, per)
        cols = pl.ds(pl.multiple_of(at * depth + t * tile, tile), tile)
        rows = hid[slot, j, :, :, :, cols].reshape(total, tile)
        return jnp.dot(left, rows, preferred_element_type=f32)

    def own_products(kv):
        left = pre_t.at[kv]

        def both(piece, t):
            return part_of(left[...].reshape(2 * HEAD_WIDTH, total), 0, piece, t)

        for w in others + [slot_w]:
            @pl.loop(0, parts)
            def _(t):
                out = both(w * CORES + 1 - core, t)
                mate_acc[kv, w, 0, t] = out[:HEAD_WIDTH]
                mate_acc[kv, w, 1, t] = out[HEAD_WIDTH:]
                out = both(w * CORES + core, t)
                acc[kv, w, 0, t] = out[:HEAD_WIDTH]
                acc[kv, w, 1, t] = out[HEAD_WIDTH:]

    def twin_products(kv, u):
        def to_mate(w):
            @pl.loop(0, parts)
            def _(t):
                v = mate_acc[kv, w, u, t] + part_of(pre_in[kv, u], 1, w * CORES + 1 - core, t)
                mate_out[kv, w, u, t] = v.astype(bf16)
                mate_copy(kv, w, u, t).start()

        def to_acc(w):
            @pl.loop(0, parts)
            def _(t):
                acc[kv, w, u, t] += part_of(pre_in[kv, u], 1, w * CORES + core, t)

        pre_copy(kv, u).wait_recv()
        for w in others:
            to_mate(w)
        for w in others:
            to_acc(w)
        for i, w in enumerate(others):
            @pl.loop(0, parts)
            def _(t):
                mate_copy(kv, w, u, t).wait_recv()
                v = acc[kv, w, u, t] + mate_in[kv, w, u, t].astype(f32)
                far_out[kv, i, u, t] = v.astype(bf16)
                far_copy(kv, i, w, u, t).start()
        to_mate(slot_w)
        to_acc(slot_w)

    def finish(kv, u):
        lanes = pl.ds(kv * HEAD_WIDTH, HEAD_WIDTH)
        grad = val_grad if u else key_grad
        for t in range(parts):
            mate_copy(kv, slot_w, u, t).wait_recv()
            v = acc[kv, slot_w, u, t] + mate_in[kv, slot_w, u, t].astype(f32)
            for i, w in enumerate(others):
                far_copy(kv, i, w, u, t, True).wait_recv()
                v = v + far_in[kv, w, u, t].astype(f32)
            grad[pl.ds(t * tile, tile), lanes] = v.T

    for c in range(4):
        e, at = stretch_of(c)
        for j in range(2):
            src = hidden.at[e, at, embed_cols(1 - side, j)]
            start(hidden_copy(1, c, j, seq, twin, seq, hid_send.at[next(slots)], src))
            for i, w in enumerate(others):
                start(far_weight(c // 2, c % 2 * 2 + j, i, w, slot_w))
    for kind in range(2):
        start(weight_copy(kind, mine, mate, mate_w_send.at[0, kind], True))
    direct(0)
    for h in range(kv_heads * group):
        for copy in own_loads(h):
            pltpu.make_async_copy(*copy).start()
    for p in range(5):
        direct(p + 1)
        relay_hidden(p)
        if p == 4:
            relay_weights(0)
    direct(6)
    relay_hidden(5)
    direct(7)
    relay_weights(1)
    for copy in loads:
        pltpu.make_async_copy(*copy).wait()
    wait_weights()
    project(2)
    project(4)
    relay_hidden(6)
    project(5)
    relay_hidden(7)
    for h in range(kv_heads * group):
        exchange(h, queries, qry, qry_send, qry_recv)
        exchange(h, out_grad, grd, grd_send, grd_recv)
    for p in (6, 0, 1, 3, 7):
        project(p)
    for kv in range(kv_heads):
        settle(kv)
        attend(kv, functools.partial(twin_products, kv - 1, 1) if kv else None)
        start(pre_copy(kv, 1))
        if kv:
            twin_products(kv - 1, 0)
        start(pre_copy(kv, 0))
        own_products(kv)
        give_back(kv)
    for u in (1, 0):
        twin_products(kv_heads - 1, u)
    for kv in range(kv_heads):
        for u in (1, 0):
            finish(kv, u)
        wait_back(kv)
    for kv in range(kv_heads):
        for u in range(2):
            for t in range(parts):
                for w in range(near):
                    mate_copy(kv, w, u, t).wait_send()
                for i, w in enumerate(others):
                    far_copy(kv, i, w, u, t).wait_send()
    for copy in sends:
        copy.wait_send()


def put_kernel(*refs):
    count = len(refs) // 2
    sem = refs[-1]
    copies = [
        pltpu.make_async_copy(refs[i], refs[count + i], sem.at[i]) for i in range(count)
    ]
    for copy in copies:
        copy.start()
    for copy in copies:
        copy.wait()


def put_all(*arrays):
    return pl.pallas_call(
        put_kernel,
        out_shape=[jax.ShapeDtypeStruct(x.shape, x.dtype) for x in arrays],
        in_specs=[pl.BlockSpec(memory_space=pltpu.VMEM)] * len(arrays),
        out_specs=[ANY] * len(arrays),
        scratch_shapes=[pltpu.SemaphoreType.DMA((len(arrays),))],
        compiler_params=pltpu.CompilerParams(vmem_limit_bytes=1 << 20),
        name="put_all",
    )(*arrays)


def local(n_seq, n_dp, hidden, queries, key_matrix, value_matrix, out_grad):
    _, stretches, tokens, embed = hidden.shape
    full = queries.shape[3]
    width = full // n_seq
    deep, kv_width = key_matrix.shape
    kv_heads = kv_width // HEAD_WIDTH
    group = width // kv_width
    wide = group * HEAD_WIDTH
    near = n_dp // CORES // 2
    quarter = embed // 4
    rows, cols = grid_of(n_seq)
    hid_sends = 8 * (2 * (rows - 1 + cols - 1) + 2 * (rows - 1) * (cols - 1)) + 8
    total = stretches * n_seq * tokens
    block = n_seq * tokens
    bf16, f32 = jnp.bfloat16, jnp.float32
    dma = pltpu.SemaphoreType.DMA
    half = HEAD_WIDTH // 2
    inverse = np.exp(
        np.arange(half, dtype=np.float32) * np.float32(-2.0 * math.log(ROPE_BASE) / HEAD_WIDTH)
    ).astype(np.float32)
    phase = np.arange(total, dtype=np.float32)[:, None] * inverse[None, :]
    cos_half, sin_half = np.cos(phase), np.sin(phase)
    cos = np.concatenate([cos_half, cos_half], axis=1).astype(np.float32)
    sin = np.concatenate([-sin_half, sin_half], axis=1).astype(np.float32)
    heads = (kv_heads, stretches, n_seq, tokens, wide)
    single = (kv_heads * group, stretches, n_seq, tokens, HEAD_WIDTH)
    tile = math.gcd(deep, TILE)
    parts = deep // tile
    blocks = (kv_heads, near, 2, parts, HEAD_WIDTH, tile)
    weights = (n_dp // 2, deep, kv_width)
    raw = (kv_heads, stretches, n_seq, tokens, HEAD_WIDTH)
    all_heads = kv_heads * group
    spare = max(near - 1, 1)
    attn_out, query_grad, key_grad, val_grad = pl.pallas_call(
        functools.partial(kernel, n_seq, n_dp, kv_heads, group, tile),
        out_shape=[
            pltpu.VMEM((stretches, tokens, full), bf16),
            pltpu.VMEM((stretches, tokens, full), bf16),
            pltpu.VMEM((deep, kv_width), f32),
            pltpu.VMEM((deep, kv_width), f32),
        ],
        in_specs=[ANY] * 9,
        out_specs=[VMEM] * 4,
        scratch_shapes=[
            pltpu.VMEM((2, 2, stretches, n_seq, tokens, quarter), bf16),
            pltpu.VMEM(single, bf16),
            pltpu.VMEM(single, bf16),
            pltpu.VMEM(weights, bf16),
            pltpu.VMEM(weights, bf16),
            pltpu.VMEM((block // 2, kv_width), f32),
            pltpu.VMEM((block // 2, kv_width), f32),
            pltpu.VMEM((2,) + raw, f32),
            pltpu.VMEM((2,) + raw, f32),
            pltpu.VMEM((2,) + raw, bf16),
            pltpu.VMEM(raw, f32),
            pltpu.VMEM(raw, bf16),
            pltpu.VMEM((total, kv_width), bf16),
            pltpu.VMEM((total, kv_width), bf16),
            pltpu.VMEM(heads, bf16),
            pltpu.VMEM(heads, bf16),
            pltpu.VMEM((kv_heads, 2, HEAD_WIDTH, total), bf16),
            pltpu.VMEM((kv_heads, 2, HEAD_WIDTH, total), bf16),
            pltpu.VMEM((HEAD_WIDTH, total), f32),
            pltpu.VMEM((HEAD_WIDTH, total), f32),
            pltpu.VMEM(blocks, f32),
            pltpu.VMEM(blocks, f32),
            pltpu.VMEM(blocks, bf16),
            pltpu.VMEM(blocks, bf16),
            pltpu.VMEM((kv_heads, spare, 2, parts, HEAD_WIDTH, tile), bf16),
            pltpu.VMEM(blocks, bf16),
            pltpu.VMEM((total, HEAD_WIDTH), f32),
            pltpu.VMEM((total, HEAD_WIDTH), f32),
            pltpu.VMEM((HEAD_WIDTH, total), f32),
            pltpu.VMEM((HEAD_WIDTH, total), f32),
            dma((6,)), dma((2, all_heads)), dma((2, kv_heads)),
            dma((hid_sends,)), dma((2, 4, 2, n_seq)),
            dma((all_heads, n_seq)), dma((all_heads, n_seq)),
            dma((all_heads, n_seq)), dma((all_heads, n_seq)),
            dma((spare, 2, 4)), dma((near, 2, 4)), dma((near, 2)), dma((n_dp // 2, 2)),
            dma((kv_heads, 4)), dma((kv_heads, 4)),
            dma((kv_heads, 4)), dma((kv_heads, 4)),
            dma((kv_heads, 2)), dma((kv_heads, 2)),
            dma((kv_heads, n_seq)), dma((kv_heads, n_seq)),
            dma((kv_heads, n_seq)), dma((kv_heads, n_seq)),
            dma((kv_heads, near, 2, parts)), dma((kv_heads, near, 2, parts)),
            dma((kv_heads, spare, 2, parts)), dma((kv_heads, near, 2, parts)),
        ],
        compiler_params=pltpu.CompilerParams(
            collective_id=0, has_side_effects=True, vmem_limit_bytes=VMEM_LIMIT
        ),
        name="attention_step",
    )(hidden[0], queries[0], key_matrix, value_matrix, out_grad[0],
      cos, sin, cos.T.copy(), sin.T.copy())
    attn_out, query_grad, key_grad, val_grad = put_all(
        attn_out, query_grad, key_grad, val_grad
    )
    return attn_out[None], query_grad[None], key_grad, val_grad


def solution(mesh):
    n_dp, n_seq = mesh.shape["dp"], mesh.shape["seq"]
    tokens, weights = P("dp", None, "seq", None), P("dp", "seq")
    return jax.shard_map(
        functools.partial(local, n_seq, n_dp),
        mesh=mesh,
        in_specs=(tokens, tokens, weights, weights, tokens),
        out_specs=(tokens, tokens, weights, weights),
        check_vma=False,
    )
```
